128 devices in a mesh: tm: 32 (over y, z, core), tmpl: 4 (over x).
Axes of the slice: x: 4, y: 4, z: 4, core: 2. Of those that a mesh axis runs over, the one named last changes fastest.
Arguments:
- waveforms: bfloat16 [2000, 131072], P(None, 'tm'), may hold values from -6 to 6
- templates: bfloat16 [64, 96, 512], P('tm', 'tmpl'), may hold values from -6 to 6
- channel_lists: int32 [64, 96], P(None, 'tmpl'), may hold values from 0 to 1999, as said below
- channel_counts: int32 [64], replicated, may hold values from 32 to 96, as said below
- owner_rounds: int32 [4], replicated, may hold values from 0 to 31
Outputs:
- detection: float32 [8, 131072], P(None, ('tm', 'tmpl'))
The draws below stay inside these ranges and needn't reach their ends.
Inputs may be any that keep to these rules, and one draw needn't show every extreme that they name: `channel_lists`: the 96 channels of one template are distinct. `channel_counts`: slots at or past a template's count are padding; at least one template uses all 96 slots.
All inputs are finite; a program needn't handle non-finite values.
Results may differ from the reference program's by a relative error of at most 0.0003.
Values may be sent and summed in bfloat16 or wider, within the bound.
No kernel may reach another device: no remote copies, remote signals or barrier semaphores. Data moves between devices by JAX's collectives and lax.ppermute only.
A program may use at most 128 MiB of HBM per device.

```python
import jax
import jax.numpy as jnp
from jax import lax

C = 2000
SLOTS = 96
L = 512
TPB = 2
ROUNDS = 4
OWNING_DEVICES = 32
NT = 64
TIME = 131072


def draw_channel_lists(key, part):
    keys = jax.random.split(jax.random.fold_in(key, 11), NT)

    def one_list(lone_entry):
        return jax.random.permutation(lone_entry, C)[:SLOTS].astype(jnp.int32)
    return jax.vmap(one_list)(keys)


def draw_channel_counts(key, part):
    base = jax.random.randint(jax.random.fold_in(key, 21), (NT,), SLOTS // 3, SLOTS + 1)
    where_full = jax.random.randint(jax.random.fold_in(key, 22), (), 0, NT)
    return jnp.where(jnp.arange(NT) == where_full, SLOTS, base).astype(jnp.int32)


def plant(array, key, least, high):
    place = [jax.random.randint(jax.random.fold_in(key, axis), (), 0, length) for axis, length in enumerate(array.shape)]
    main_axis = array.shape.index(max(array.shape))
    beside = place[:main_axis] + [(place[main_axis] + 1) % array.shape[main_axis]] + place[main_axis + 1:]
    return array.at[tuple(place)].set(least).at[tuple(beside)].set(high)


def steps_of(key, shape, cuts, smallest, high):
    def one(dim, shards_of):
        heights = jax.random.uniform(jax.random.fold_in(jax.random.fold_in(key, 6), dim), (shards_of,), jnp.float32, smallest / len(cuts), high / len(cuts))
        return jnp.repeat(jnp.exp(heights), shape[dim] // shards_of).reshape((-1,) + (1,) * (len(shape) - dim - 1))

    factor_of = one(*cuts[0])
    for cut in cuts[1:]:
        factor_of = factor_of * one(*cut)
    return factor_of


def noise(own_key, dims, spread, bound, shards=(), held_as=jnp.bfloat16):
    result = jax.random.normal(own_key, dims, jnp.float32) * spread
    if len(shards) > 0:
        result = steps_of(own_key, dims, shards, -0.22, 0.18) * result
    return jnp.clip(result, min=-bound, max=bound).astype(held_as)


def setup_inputs(seed: int = 0) -> dict:
    streams_of = jax.random.split(jax.random.key(seed), 6)
    waveforms = noise(streams_of[0], (C, TIME), 1.0, 6.0, ((1, 32),))
    templates = noise(streams_of[1], (NT, SLOTS, L), 1.0, 6.0, ((0, 32), (1, 4)))
    channel_lists = draw_channel_lists(jax.random.fold_in(streams_of[5], 71), 0)
    channel_counts = draw_channel_counts(jax.random.fold_in(streams_of[5], 71), 0)
    owner_rounds = plant(jax.random.randint(streams_of[4], (ROUNDS,), 0, OWNING_DEVICES), jax.random.fold_in(streams_of[4], 1), 0, OWNING_DEVICES - 1).astype(jnp.int32)
    return {"waveforms": waveforms, "templates": templates, "channel_lists": channel_lists, "channel_counts": channel_counts, "owner_rounds": owner_rounds}


stability_floor = 1e-06

def reference(waveforms, templates, channel_lists, channel_counts, owner_rounds):
    fft_len = 2 * TIME

    def one_template(template_id):
        chosen = lax.dynamic_index_in_dim(channel_lists, template_id, 0, keepdims=False)
        picked = jnp.take(waveforms, chosen, axis=0).astype(jnp.float32)
        waveset = lax.dynamic_index_in_dim(templates, template_id, 0, keepdims=False).astype(jnp.float32)
        spectrum = jnp.fft.rfft(picked, n=fft_len, axis=1)
        tmpl_spectrum = jnp.fft.rfft(waveset, n=fft_len, axis=1)
        correl = jnp.fft.irfft(spectrum * jnp.conj(tmpl_spectrum), n=fft_len, axis=1)[:, :TIME]
        squares = jnp.pad(picked * picked, ((0, 0), (0, L)))
        running = jnp.concatenate([jnp.zeros((SLOTS, 1), jnp.float32), jnp.cumsum(squares, axis=1)], axis=1)
        energy = running[:, L:L + TIME] - running[:, :TIME]
        template_power = lax.optimization_barrier(jnp.sum(waveset * waveset, axis=1))
        normed = correl / (jnp.sqrt(jnp.maximum(energy, L / 4.0)) * jnp.sqrt(template_power + stability_floor)[:, None])
        current_count = lax.dynamic_index_in_dim(channel_counts, template_id, 0, keepdims=False)
        usable = jnp.arange(SLOTS, dtype=jnp.int32) < current_count
        return lax.optimization_barrier(jnp.sum(jnp.where(usable[:, None], normed, 0.0), axis=0))
    template_ids = (owner_rounds[:, None] * TPB + jnp.arange(TPB, dtype=jnp.int32)[None, :]).reshape(-1).astype(jnp.int32)
    return lax.map(one_template, template_ids)
```

```python
import functools

import jax
import jax.numpy as jnp
from jax import lax
from jax.experimental import pallas as pl
from jax.experimental.pallas import tpu as pltpu
from jax.sharding import PartitionSpec as P

bf=jnp.bfloat16; f32=jnp.float32
NB=32; YB=40
def head_kernel(slots, owner, cl, wf, o, buf, scr, sem):
    n=buf.shape[0]
    def ch(i):
        j=i//slots
        return cl[owner[j//2]*2+j%2, i%slots]
    def cp(i,c):
        r=pl.multiple_of(((c%8)//2)*2,2)
        return pltpu.make_async_copy(wf.at[c//8,pl.ds(0,4),pl.ds(r,2),:], buf.at[i], sem.at[0])
    def start(i,_): cp(i,ch(i)).start(); return 0
    def wait(i,_): cp(i,0).wait(); return 0
    lax.fori_loop(0,n,start,0,unroll=8)
    lax.fori_loop(0,n,wait,0,unroll=8)
    G=8
    def body(g,_):
        scr[...]=buf[pl.ds(g*G,G)].reshape(G*8,128).astype(f32)
        for k in range(G):
            i=g*G+k
            o[pl.ds(i*4,4),:]=scr[pl.ds(k*8+ch(i)%2,4,stride=2),:]
        return 0
    lax.fori_loop(0,n//G,body,0)
def corr_kernel(slots, w_ref, y_ref, rn_ref, cnt_ref, o_ref, w32, sc):
    n=w_ref.shape[0]; nt=n//slots
    w=w_ref[...].astype(f32)
    for j in range(4): w32[j]=w[:,128*j:128*(j+1)]
    q=w*w
    hi=q.astype(bf); lo=(q-hi.astype(f32)).astype(bf)
    ones=jnp.ones((512,128),bf)
    te=jnp.dot(hi,ones,preferred_element_type=f32)+jnp.dot(lo,ones,preferred_element_type=f32)
    sc[...]=cnt_ref[...]*lax.rsqrt(te+1e-6)
    lane=lax.broadcasted_iota(jnp.int32,(128,128),1); row=lax.broadcasted_iota(jnp.int32,(128,128),0)
    up=lane>=row
    zero=jnp.zeros((128,128),f32)
    def one(i):
        R=[]
        for j in range(4):
            b=w32[j,pl.ds(i,8,stride=0),:]
            b=jnp.concatenate([b]*16,axis=0)
            R.append(pltpu.roll(b,0,axis=1,stride=1,stride_axis=0))
        R=[zero]+R+[zero]
        T=jnp.concatenate([jnp.where(up,R[j+1],R[j]).astype(bf) for j in range(5)],axis=1)
        X=jnp.concatenate([y_ref[i,j:j+32,:].astype(bf) for j in range(5)],axis=1)
        out=lax.dot_general(X,T,(((1,),(1,)),((),())),preferred_element_type=f32)
        s=sc[pl.ds(i,8,stride=0),:]
        return out*rn_ref[i]*jnp.concatenate([s]*4,axis=0)
    for t in range(nt):
        def body(k,acc):
            return acc+one(t*slots+k)
        o_ref[t]=lax.fori_loop(0,slots,body,jnp.zeros((32,128),f32),unroll=UN)
UN=2
def corr(w,y,rn,cnt,slots=24):
    n=w.shape[0]
    return pl.pallas_call(functools.partial(corr_kernel,slots),
      out_shape=jax.ShapeDtypeStruct((n//slots,32,128),f32),
      scratch_shapes=[pltpu.VMEM((4,n,128),f32),pltpu.VMEM((n,128),f32)],
      compiler_params=pltpu.CompilerParams(vmem_limit_bytes=60*1024*1024))(w,y,rn,cnt)
def heads(owner,cl,wf4,slots=24,n=192):
    return pl.pallas_call(functools.partial(head_kernel,slots),
      out_shape=jax.ShapeDtypeStruct((n*4,128),f32),
      grid_spec=pltpu.PrefetchScalarGridSpec(num_scalar_prefetch=2,grid=(),in_specs=[pl.BlockSpec(memory_space=pl.ANY)],
        out_specs=pl.BlockSpec(memory_space=pltpu.VMEM),
        scratch_shapes=[pltpu.VMEM((n,4,2,128),bf),pltpu.VMEM((64,128),f32),pltpu.SemaphoreType.DMA((1,))]))(owner,cl,wf4)
def energy_kernel(slots, owner, cl, wf, hd, y, rn, buf, scr, pt, sem):
    n=buf.shape[0]
    def ch(i):
        j=i//slots
        return cl[owner[j//2]*2+j%2, i%slots]
    def cp(i,c):
        r=pl.multiple_of(((c%8)//2)*2,2)
        return pltpu.make_async_copy(wf.at[c//8,:,pl.ds(r,2),:], buf.at[i], sem.at[i])
    def start(i,_): cp(i,ch(i)).start(); return 0
    lax.fori_loop(0,n,start,0,unroll=8)
    r0=lax.broadcasted_iota(jnp.int32,(256,256),0)%128; c0=lax.broadcasted_iota(jnp.int32,(256,256),1)
    U=jnp.where((c0>=128)|(r0<c0),1.0,0.0).astype(bf)
    G=EG
    def body(g,_):
        for k in range(G):
            i=g*G+k
            cp(i,0).wait()
            scr[k]=buf[i].reshape(64,128).astype(f32)
        sqs=[]
        for k in range(G):
            i=g*G+k
            a=scr[k,pl.ds(ch(i)%2,32,stride=2),:]
            y[i,0:32,:]=a
            y[i,32:36,:]=hd[pl.ds(i*4,4),:]
            y[i,36:40,:]=jnp.zeros((4,128),f32)
            a=y[i]
            sqs.append(a*a)
        q=jnp.concatenate(sqs,axis=0)
        hi=q.astype(bf); lo=(q-hi.astype(f32)).astype(bf)
        pt[...]=jnp.dot(jnp.concatenate([hi,lo],axis=1),U,preferred_element_type=f32)
        for k in range(G):
            o=k*YB
            tot=[pt[o+d:o+d+32,128:256] for d in range(4)]
            e=(tot[0]+tot[1])+(tot[2]+tot[3])+(pt[o+4:o+36,0:128]-pt[o:o+32,0:128])
            rn[g*G+k]=lax.rsqrt(jnp.maximum(e,128.0))
        return 0
    lax.fori_loop(0,n//G,body,0)
EG=8
def energy(owner,cl,wf4,hd,slots=24,n=192):
    return pl.pallas_call(functools.partial(energy_kernel,slots),
      out_shape=(jax.ShapeDtypeStruct((n,YB,128),f32),jax.ShapeDtypeStruct((n,32,128),f32)),
      grid_spec=pltpu.PrefetchScalarGridSpec(num_scalar_prefetch=2,grid=(),in_specs=[pl.BlockSpec(memory_space=pl.ANY),pl.BlockSpec(memory_space=pltpu.VMEM)],
        out_specs=(pl.BlockSpec(memory_space=pltpu.VMEM),pl.BlockSpec(memory_space=pltpu.VMEM)),
        scratch_shapes=[pltpu.VMEM((n,32,2,128),bf),pltpu.VMEM((EG,64,128),f32),pltpu.VMEM((EG*YB,256),f32),pltpu.SemaphoreType.DMA((n,))]),
      compiler_params=pltpu.CompilerParams(vmem_limit_bytes=60*1024*1024))(owner,cl,wf4,hd)


def permuted(x, axis, to):
    return lax.ppermute(x, axis, [(i, to(i)) for i in range(lax.axis_size(axis))])


def shards(waveforms, templates, channel_lists, channel_counts, owner_rounds):
    c, shard_len = waveforms.shape
    tpb, slots, taps = templates.shape
    rounds = owner_rounds.shape[0]
    nt = rounds * tpb
    n = nt * slots
    me = lax.axis_index("tm")
    group = lax.axis_index("tmpl")
    wf4 = waveforms.reshape(c // 8, 8, shard_len // 128, 128).transpose(0, 2, 1, 3)
    mine = (owner_rounds == me)[:, None, None, None]
    waves = jnp.where(mine, templates[None], jnp.zeros((), templates.dtype)).reshape(n, taps)
    for s in (1, 2, 4, 8, 16):
        waves = waves + permuted(waves, "tm", lambda i, s=s: i ^ s)
    hd = heads(owner_rounds, channel_lists, wf4, slots, n).astype(jnp.bfloat16)
    hd = lax.ppermute(hd, "tm", [(i, i - 1) for i in range(1, lax.axis_size("tm"))]).astype(jnp.float32)
    y, rn = energy(owner_rounds, channel_lists, wf4, hd, slots, n)
    ids = (owner_rounds[:, None] * tpb + jnp.arange(tpb, dtype=jnp.int32)[None, :]).reshape(-1)
    counts = jnp.take(channel_counts, ids, axis=0)
    slot_ids = group * slots + jnp.arange(slots, dtype=jnp.int32)
    mask = jnp.broadcast_to((slot_ids[None, :] < counts[:, None]).astype(jnp.float32).reshape(n, 1), (n, 128))
    local = corr(waves, y, rn, mask, slots)
    groups = lax.axis_size("tmpl")
    local = local.reshape(nt, groups, shard_len // groups)
    pick = lambda k: lax.dynamic_index_in_dim(local, (group + k) % groups, 1, keepdims=False)
    out = pick(0)
    for k in range(1, groups):
        out = out + lax.ppermute(pick(k), "tmpl", [(i, (i + k) % groups) for i in range(groups)])
    return out


def solution(mesh):
    in_specs = (P(None, "tm"), P("tm", "tmpl", None), P(None, "tmpl"), P(), P())
    return jax.shard_map(shards, mesh=mesh, in_specs=in_specs, out_specs=P(None, ("tm", "tmpl")), check_vma=False)
```

```python
import functools

import jax
import jax.numpy as jnp
from jax import lax
from jax.experimental import pallas as pl
from jax.experimental.pallas import tpu as pltpu
from jax.sharding import PartitionSpec as P

bf16, f32, i32 = jnp.bfloat16, jnp.float32, jnp.int32
LANES = 128
FLOOR = 1e-6
GROUP = 8
UNROLL = 12
VMEM_LIMIT = 24 * 1024 * 1024


def vmem_spec():
    return pl.BlockSpec(memory_space=pltpu.VMEM)


def smem_spec():
    return pl.BlockSpec(memory_space=pltpu.SMEM)


def exact_pair(x):
    hi = x.astype(bf16)
    return hi, (x - hi.astype(f32)).astype(bf16)


def gather_kernel(tpb, owner, lists, wf, y, heads, buf, scr, hs, sem):
    slots = lists.shape[0]
    n, blocks = y.shape[0], y.shape[1]
    hb = heads.shape[0] // n

    def template(t):
        return owner[t // tpb] * tpb + t % tpb

    def copy(i, c):
        pair = pl.multiple_of(((c % 8) // 2) * 2, 2)
        return pltpu.make_async_copy(wf.at[c // 8, :, pl.ds(pair, 2), :], buf.at[i], sem.at[i])

    for t in range(n // slots):
        tid = template(t)

        def start(s, _, t=t, tid=tid):
            copy(t * slots + s, lists[s, tid]).start()
            return 0

        lax.fori_loop(0, slots, start, 0, unroll=8)

    for t in range(n // slots):
        tid = template(t)

        def group(g, _, t=t, tid=tid):
            for k in range(GROUP):
                s = g * GROUP + k
                copy(t * slots + s, 0).wait()
            for k in range(GROUP):
                s = g * GROUP + k
                i = t * slots + s
                scr[k, 0 : 2 * blocks, :] = buf[i].reshape(2 * blocks, LANES).astype(f32)
                own = scr[k, pl.ds(lists[s, tid] % 2, blocks, stride=2), :]
                y[i] = own
                hs[pl.ds(i * hb, hb), :] = own[0:hb]
            return 0

        lax.fori_loop(0, slots // GROUP, group, 0)
    heads[...] = hs[...].astype(bf16)


def energy_kernel(taps, y, halo, rn, a, yg, pg, tg):
    n, blocks = y.shape[0], y.shape[1]
    tb = taps // LANES
    rows = yg.shape[1]
    half = blocks // 2
    wide = 2 * LANES
    r = lax.broadcasted_iota(i32, (wide, wide), 0) % LANES
    c = lax.broadcasted_iota(i32, (wide, wide), 1)
    sums = jnp.where((c >= LANES) | (r < c), 1.0, 0.0).astype(bf16)
    for k in range(GROUP):
        yg[k, blocks + tb :, :] = jnp.zeros((rows - blocks - tb, LANES), f32)

    def group(g, _):
        tails = halo[pl.ds(pl.multiple_of(g * GROUP * tb, GROUP * tb), GROUP * tb), :].astype(f32)
        for k in range(GROUP):
            yg[k, 0:blocks, :] = y[g * GROUP + k]
            yg[k, blocks : blocks + tb, :] = tails[tb * k : tb * (k + 1)]
        q = yg[...].reshape(GROUP * rows, LANES)
        parts = jnp.dot(jnp.concatenate(exact_pair(q * q), axis=1), sums, preferred_element_type=f32)
        pg[0 : GROUP * rows, :] = parts[:, 0:LANES]
        tg[0 : GROUP * rows, :] = parts[:, LANES:]
        for k in range(GROUP):
            i = g * GROUP + k
            o = k * rows
            tot = [tg[pl.ds(o + d, half, stride=2), :] for d in range(tb + 1)]
            pre = [pg[pl.ds(o + d, half, stride=2), :] for d in (0, 1, tb, tb + 1)]
            for v in range(2):
                e = pre[2 + v] - pre[v]
                for d in range(tb):
                    e = e + tot[v + d]
                rn[i, half * v : half * (v + 1), :] = lax.rsqrt(jnp.maximum(e, taps / 4.0))
            for v in range(tb + 2):
                a[i, half * v : half * (v + 1), :] = yg[k, pl.ds(v, half, stride=2), :].astype(bf16)
        return 0

    lax.fori_loop(0, n // GROUP, group, 0)


def correlate_kernel(tpb, slots, owner, counts, place, w, a, rn, *refs):
    outs, (wr, scale, acc) = refs[:-3], refs[-3:]
    n, taps = w.shape
    tb = taps // LANES
    nt = n // slots
    blocks = rn.shape[1]
    half = blocks // 2
    parts = len(outs)
    group = place[0]
    wf = w[...].astype(f32)
    hi, lo = exact_pair(wf * wf)
    ones = jnp.ones((taps, LANES), bf16)
    power = jnp.dot(hi, ones, preferred_element_type=f32) + jnp.dot(lo, ones, preferred_element_type=f32)
    norm = lax.rsqrt(power + FLOOR)
    slot_ids = lax.broadcasted_iota(i32, (slots, LANES), 0) + group * slots
    for t in range(nt):
        count = counts[owner[t // tpb] * tpb + t % tpb]
        scale[t * slots : (t + 1) * slots, :] = jnp.where(slot_ids < count, norm[t * slots : (t + 1) * slots], 0.0)
    row = lax.broadcasted_iota(i32, (LANES, LANES), 0)
    col = lax.broadcasted_iota(i32, (LANES, LANES), 1)
    flip = jnp.where(row + col == LANES - 1, 1.0, 0.0).astype(bf16)
    for j in range(tb):
        wr[j, 0:n, :] = jnp.dot(w[:, LANES * j : LANES * (j + 1)], flip, preferred_element_type=f32)
    own = row >= col
    zero = jnp.zeros((LANES, LANES), bf16)

    def one(i):
        d = [zero]
        for j in range(tb):
            b = jnp.concatenate([wr[j, pl.ds(i, 8, stride=0), :]] * (LANES // 8), axis=0)
            d.append(pltpu.roll(b, 1, axis=1, stride=1, stride_axis=0).astype(bf16))
        d.append(zero)
        band = jnp.concatenate([jnp.where(own, d[j + 1], d[j]) for j in range(tb + 1)], axis=0)
        x = jnp.concatenate([a[i, half * j : half * (j + 2), :] for j in range(tb + 1)], axis=1)
        out = jnp.dot(x, band, preferred_element_type=f32)
        s = scale[pl.ds(i, 8, stride=0), :]
        return out * rn[i] * jnp.concatenate([s] * (blocks // 8), axis=0)

    def template(t, _):
        r = lax.fori_loop(
            0, slots, lambda k, total: total + one(t * slots + k), jnp.zeros((blocks, LANES), f32), unroll=UNROLL
        )
        for v in range(2):
            acc[pl.ds(v * nt + t, half, stride=2 * nt), :] = r[half * v : half * (v + 1)]
        return 0

    lax.fori_loop(0, nt, template, 0)
    per = blocks // parts
    for k, o in enumerate(outs):
        to = (group + k) % parts
        for b in range(per):
            o[:, LANES * b : LANES * (b + 1)] = acc[pl.ds(pl.multiple_of((to * per + b) * nt, 8), nt), :]


def gather(owner, lists, wf4, tpb, tb):
    slots = lists.shape[0]
    n = owner.shape[0] * tpb * slots
    blocks = wf4.shape[1]
    return pl.pallas_call(
        functools.partial(gather_kernel, tpb),
        out_shape=(pltpu.VMEM((n, blocks, LANES), f32), jax.ShapeDtypeStruct((n * tb, LANES), bf16)),
        in_specs=[smem_spec(), smem_spec(), pl.BlockSpec(memory_space=pltpu.HBM)],
        out_specs=(vmem_spec(), vmem_spec()),
        scratch_shapes=[
            pltpu.VMEM((n, blocks, 2, LANES), bf16),
            pltpu.VMEM((GROUP, 2 * blocks + 8, LANES), f32),
            pltpu.VMEM((n * tb, LANES), f32),
            pltpu.SemaphoreType.DMA((n,)),
        ],
        compiler_params=pltpu.CompilerParams(vmem_limit_bytes=VMEM_LIMIT),
        name="gather_rows",
    )(owner, lists, pltpu.with_memory_space_constraint(wf4, pltpu.HBM))


def energy(y, halo, taps):
    n, blocks, _ = y.shape
    tb = taps // LANES
    rows = blocks + 8
    return pl.pallas_call(
        functools.partial(energy_kernel, taps),
        out_shape=(pltpu.VMEM((n, blocks, LANES), f32), pltpu.VMEM((n, blocks // 2 * (tb + 2), LANES), bf16)),
        in_specs=[vmem_spec(), vmem_spec()],
        out_specs=(vmem_spec(), vmem_spec()),
        scratch_shapes=[
            pltpu.VMEM((GROUP, rows, LANES), f32),
            pltpu.VMEM((GROUP * rows + 8, LANES), f32),
            pltpu.VMEM((GROUP * rows + 8, LANES), f32),
        ],
        compiler_params=pltpu.CompilerParams(vmem_limit_bytes=VMEM_LIMIT),
        name="window_energy",
    )(y, halo)


def correlate(owner, counts, place, w, a, rn, tpb, slots, parts):
    n, taps = w.shape
    nt = n // slots
    blocks = rn.shape[1]
    return pl.pallas_call(
        functools.partial(correlate_kernel, tpb, slots),
        out_shape=tuple(jax.ShapeDtypeStruct((nt, blocks // parts * LANES), f32) for _ in range(parts)),
        in_specs=[smem_spec()] * 3 + [vmem_spec()] * 3,
        out_specs=tuple(vmem_spec() for _ in range(parts)),
        scratch_shapes=[
            pltpu.VMEM((taps // LANES, n + 8, LANES), f32),
            pltpu.VMEM((n + 8, LANES), f32),
            pltpu.VMEM(((blocks + 2) * nt, LANES), f32),
        ],
        compiler_params=pltpu.CompilerParams(vmem_limit_bytes=VMEM_LIMIT),
        name="correlate",
    )(owner, counts, place, w, a, rn)


def turned(i, dy, dz):
    return ((i // 8 + dy) % 4) * 8 + ((i // 2 + dz) % 4) * 2 + i % 2


def sent(x, to):
    return lax.ppermute(x, "tm", [(i, to(i)) for i in range(32)])


def round_the_ring(x, first):
    total = x
    for k in (1, 3, 2):
        total = total + sent(x, lambda i: turned(i, 0, k) if (i % 2 == 0) == first else turned(i, k, 0))
    return total


def shards(waveforms, templates, channel_lists, channel_counts, owner_rounds):
    c, shard_len = waveforms.shape
    tpb, slots, taps = templates.shape
    rounds = owner_rounds.shape[0]
    n = rounds * tpb * slots
    me = lax.axis_index("tm")
    group = lax.axis_index("tmpl")
    groups = lax.axis_size("tmpl")
    wf4 = waveforms.reshape(c // 8, 8, shard_len // LANES, LANES).transpose(0, 2, 1, 3)
    other = sent(templates, lambda i: i ^ 1)
    owned = (owner_rounds == me)[:, None, None, None]
    paired = (owner_rounds == (me ^ 1))[:, None, None, None]
    nil = jnp.zeros((), templates.dtype)
    waves = jnp.where(owned, templates[None], jnp.where(paired, other[None], nil)).reshape(n, taps)
    waves = round_the_ring(waves, True)
    y, heads = gather(owner_rounds, channel_lists.T, wf4, tpb, taps // LANES)
    halo = lax.ppermute(heads, "tm", [(i, i - 1) for i in range(1, 32)])
    waves = round_the_ring(waves, False)
    rn, a = energy(y, halo, taps)
    pieces = correlate(owner_rounds, channel_counts, group.reshape(1), waves, a, rn, tpb, slots, groups)
    out = pieces[0]
    for k in range(1, groups):
        out = out + lax.ppermute(pieces[k], "tmpl", [(i, (i + k) % groups) for i in range(groups)])
    return out


def solution(mesh):
    in_specs = (P(None, "tm"), P("tm", "tmpl", None), P(None, "tmpl"), P(), P())
    return jax.shard_map(shards, mesh=mesh, in_specs=in_specs, out_specs=P(None, ("tm", "tmpl")), check_vma=False)
```

```python
import functools

import jax
import jax.numpy as jnp
from jax import lax
from jax.experimental import pallas as pl
from jax.experimental.pallas import tpu as pltpu
from jax.sharding import PartitionSpec as P

bf16, f32, i32 = jnp.bfloat16, jnp.float32, jnp.int32
LANES = 128
FLOOR = 1e-6
GROUP = 8
UNROLL = 12
VMEM_LIMIT = 12 * 1024 * 1024


def in_hbm(x):
    return pltpu.with_memory_space_constraint(x, pltpu.HBM)


def vmem_spec():
    return pl.BlockSpec(memory_space=pltpu.VMEM)


def exact_pair(x):
    hi = x.astype(bf16)
    return hi, (x - hi.astype(f32)).astype(bf16)


def chosen(owner, lists, tpb, t, s):
    return lists[s, owner[lax.div(t, tpb)] * tpb + lax.rem(t, tpb)]


def gather_kernel(tpb, owner, lists, wf, pairs, heads, scr, hs, sem):
    slots = lists.shape[0]
    n = pairs.shape[0]
    hb = heads.shape[0] // n

    def copy(i, c):
        pair = pl.multiple_of((c & 6), 2)
        return pltpu.make_async_copy(wf.at[c >> 3, :, pl.ds(pair, 2), :], pairs.at[i], sem.at[i])

    def start(t, _):
        def one(s, _):
            copy(t * slots + s, chosen(owner, lists, tpb, t, s)).start()
            return 0

        return lax.fori_loop(0, slots, one, 0, unroll=8)

    lax.fori_loop(0, n // slots, start, 0)

    def pick(t, _):
        def group(g, _):
            i = t * slots + g * GROUP
            for k in range(GROUP):
                copy(i + k, 0).wait()
            scr[0 : GROUP * 2 * hb, :] = pairs[pl.ds(i, GROUP), 0:hb].reshape(GROUP * 2 * hb, LANES).astype(f32)
            for k in range(GROUP):
                p = chosen(owner, lists, tpb, t, g * GROUP + k) & 1
                hs[pl.ds((i + k) * hb, hb), :] = scr[pl.ds(2 * hb * k + p, hb, stride=2), :]
            return 0

        return lax.fori_loop(0, slots // GROUP, group, 0)

    lax.fori_loop(0, n // slots, pick, 0)
    heads[...] = hs[...].astype(bf16)


def energy_kernel(tpb, taps, owner, lists, pairs, halo, rn, a, scr, band):
    slots = lists.shape[0]
    n, blocks = rn.shape[0], rn.shape[1]
    tb = taps // LANES
    half = blocks // 2
    l = lax.broadcasted_iota(i32, (LANES, LANES), 0)
    c = lax.broadcasted_iota(i32, (LANES, LANES), 1)
    first = jnp.where(l >= c, 1.0, 0.0).astype(bf16)
    last = jnp.where(l < c, 1.0, 0.0).astype(bf16)
    for k, piece in enumerate((first, first, jnp.ones_like(first), jnp.ones_like(first), last, last)):
        band[LANES * k : LANES * (k + 1), :] = piece

    def template(t, _):
        def group(g, _):
            base = t * slots + g * GROUP
            tails = halo[pl.ds(pl.multiple_of(base * tb, GROUP * tb), GROUP * tb), :].astype(f32)
            lhs = []
            for k in range(GROUP):
                i = base + k
                p = chosen(owner, lists, tpb, t, g * GROUP + k) & 1
                scr[k, 0 : 2 * blocks, :] = pairs[i].reshape(2 * blocks, LANES).astype(f32)
                scr[k, pl.ds(2 * blocks + p, tb, stride=2), :] = tails[tb * k : tb * (k + 1)]
                q = []
                for v in range(tb + 2):
                    x = scr[k, pl.ds(2 * v + p, half, stride=4), :]
                    a[i, half * v : half * (v + 1), :] = x.astype(bf16)
                    q.append(x * x)
                for v in range(2):
                    mid = functools.reduce(jnp.add, [q[v + d] for d in range(1, tb)])
                    lhs.append(jnp.concatenate(sum((exact_pair(z) for z in (q[v], mid, q[v + tb])), ()), axis=1))
            e = jnp.dot(jnp.concatenate(lhs, axis=0), band[...], preferred_element_type=f32)
            e = lax.rsqrt(jnp.maximum(e, taps / 4.0))
            for k in range(GROUP):
                rn[base + k] = e[blocks * k : blocks * (k + 1)]
            return 0

        return lax.fori_loop(0, slots // GROUP, group, 0)

    lax.fori_loop(0, n // slots, template, 0)


def correlate_kernel(tpb, slots, owner, counts, place, w, a, rn, *refs):
    outs, (wr, scale, acc) = refs[:-3], refs[-3:]
    n, taps = w.shape
    tb = taps // LANES
    nt = n // slots
    blocks = rn.shape[1]
    half = blocks // 2
    parts = len(outs)
    group = place[0]
    wf = w[...].astype(f32)
    hi, lo = exact_pair(wf * wf)
    ones = jnp.ones((taps, LANES), bf16)
    power = jnp.dot(hi, ones, preferred_element_type=f32) + jnp.dot(lo, ones, preferred_element_type=f32)
    norm = lax.rsqrt(power + FLOOR)
    slot_ids = lax.broadcasted_iota(i32, (slots, LANES), 0) + group * slots
    for t in range(nt):
        count = counts[owner[t // tpb] * tpb + t % tpb]
        scale[t * slots : (t + 1) * slots, :] = jnp.where(slot_ids < count, norm[t * slots : (t + 1) * slots], 0.0)
    row = lax.broadcasted_iota(i32, (LANES, LANES), 0)
    col = lax.broadcasted_iota(i32, (LANES, LANES), 1)
    flip = jnp.where(row + col == LANES - 1, 1.0, 0.0).astype(bf16)
    for j in range(tb):
        wr[j, 0:n, :] = jnp.dot(w[:, LANES * j : LANES * (j + 1)], flip, preferred_element_type=f32)
    own = row >= col
    zero = jnp.zeros((LANES, LANES), bf16)

    def one(i):
        d = [zero]
        for j in range(tb):
            b = jnp.concatenate([wr[j, pl.ds(i, 8, stride=0), :]] * (LANES // 8), axis=0)
            d.append(pltpu.roll(b, 1, axis=1, stride=1, stride_axis=0).astype(bf16))
        d.append(zero)
        band = jnp.concatenate([jnp.where(own, d[j + 1], d[j]) for j in range(tb + 1)], axis=0)
        x = jnp.concatenate([a[i, half * j : half * (j + 2), :] for j in range(tb + 1)], axis=1)
        out = jnp.dot(x, band, preferred_element_type=f32)
        s = scale[pl.ds(i, 8, stride=0), :]
        return out * rn[i] * jnp.concatenate([s] * (blocks // 8), axis=0)

    def template(t, _):
        r = lax.fori_loop(
            0, slots, lambda k, total: total + one(t * slots + k), jnp.zeros((blocks, LANES), f32), unroll=UNROLL
        )
        for v in range(2):
            acc[pl.ds(v * nt + t, half, stride=2 * nt), :] = r[half * v : half * (v + 1)]
        return 0

    lax.fori_loop(0, nt, template, 0)
    per = blocks // parts
    for k, o in enumerate(outs):
        to = (group + k) % parts
        for b in range(per):
            o[:, LANES * b : LANES * (b + 1)] = acc[pl.ds(pl.multiple_of((to * per + b) * nt, 8), nt), :]


def gather(owner, lists, wf4, tpb, tb):
    slots = lists.shape[0]
    n = owner.shape[0] * tpb * slots
    blocks = wf4.shape[1]
    return pl.pallas_call(
        functools.partial(gather_kernel, tpb),
        out_shape=(pltpu.VMEM((n, blocks, 2, LANES), bf16), jax.ShapeDtypeStruct((n * tb, LANES), bf16)),
        grid_spec=pltpu.PrefetchScalarGridSpec(
            num_scalar_prefetch=2,
            in_specs=[pl.BlockSpec(memory_space=pltpu.HBM)],
            out_specs=(vmem_spec(), vmem_spec()),
            scratch_shapes=[
                pltpu.VMEM((GROUP * 2 * tb + 8, LANES), f32),
                pltpu.VMEM((n * tb, LANES), f32),
                pltpu.SemaphoreType.DMA((n,)),
            ],
        ),
        compiler_params=pltpu.CompilerParams(vmem_limit_bytes=VMEM_LIMIT),
        name="gather_rows",
    )(in_hbm(owner), in_hbm(lists), in_hbm(wf4))


def energy(owner, lists, pairs, halo, tpb, taps):
    n, blocks = pairs.shape[0], pairs.shape[1]
    tb = taps // LANES
    return pl.pallas_call(
        functools.partial(energy_kernel, tpb, taps),
        out_shape=(pltpu.VMEM((n, blocks, LANES), f32), pltpu.VMEM((n, blocks // 2 * (tb + 2), LANES), bf16)),
        grid_spec=pltpu.PrefetchScalarGridSpec(
            num_scalar_prefetch=2,
            in_specs=[vmem_spec(), vmem_spec()],
            out_specs=(vmem_spec(), vmem_spec()),
            scratch_shapes=[
                pltpu.VMEM((GROUP, 2 * (blocks + tb) + 8, LANES), f32),
                pltpu.VMEM((6 * LANES, LANES), bf16),
            ],
        ),
        compiler_params=pltpu.CompilerParams(vmem_limit_bytes=VMEM_LIMIT),
        name="window_energy",
    )(in_hbm(owner), in_hbm(lists), pairs, halo)


def correlate(owner, counts, place, w, a, rn, tpb, slots, parts):
    n, taps = w.shape
    nt = n // slots
    blocks = rn.shape[1]
    return pl.pallas_call(
        functools.partial(correlate_kernel, tpb, slots),
        out_shape=tuple(jax.ShapeDtypeStruct((nt, blocks // parts * LANES), f32) for _ in range(parts)),
        grid_spec=pltpu.PrefetchScalarGridSpec(
            num_scalar_prefetch=3,
            in_specs=[vmem_spec()] * 3,
            out_specs=tuple(vmem_spec() for _ in range(parts)),
            scratch_shapes=[
                pltpu.VMEM((taps // LANES, n + 8, LANES), f32),
                pltpu.VMEM((n + 8, LANES), f32),
                pltpu.VMEM(((blocks + 2) * nt, LANES), f32),
            ],
        ),
        compiler_params=pltpu.CompilerParams(vmem_limit_bytes=VMEM_LIMIT),
        name="correlate",
    )(in_hbm(owner), in_hbm(counts), place, w, a, rn)


def turned(i, dy, dz):
    return ((i // 8 + dy) % 4) * 8 + ((i // 2 + dz) % 4) * 2 + i % 2


def sent(x, to):
    return lax.ppermute(x, "tm", [(i, to(i)) for i in range(32)])


def round_the_ring(x, first):
    total = x
    for k in (1, 3, 2):
        total = total + sent(x, lambda i: turned(i, 0, k) if (i % 2 == 0) == first else turned(i, k, 0))
    return total


def shards(waveforms, templates, channel_lists, channel_counts, owner_rounds):
    c, shard_len = waveforms.shape
    tpb, slots, taps = templates.shape
    rounds = owner_rounds.shape[0]
    n = rounds * tpb * slots
    me = lax.axis_index("tm")
    group = lax.axis_index("tmpl")
    groups = lax.axis_size("tmpl")
    wf4 = waveforms.reshape(c // 8, 8, shard_len // LANES, LANES).transpose(0, 2, 1, 3)
    other = sent(templates, lambda i: i ^ 1)
    owned = (owner_rounds == me)[:, None, None, None]
    paired = (owner_rounds == (me ^ 1))[:, None, None, None]
    nil = jnp.zeros((), templates.dtype)
    waves = jnp.where(owned, templates[None], jnp.where(paired, other[None], nil)).reshape(n, taps)
    waves = round_the_ring(waves, True)
    lists = channel_lists.T
    pairs, heads = gather(owner_rounds, lists, wf4, tpb, taps // LANES)
    heads, waves = lax.optimization_barrier((heads, waves))
    halo = lax.ppermute(heads, "tm", [(i, i - 1) for i in range(1, 32)])
    waves = round_the_ring(waves, False)
    rn, a = energy(owner_rounds, lists, pairs, halo, tpb, taps)
    pieces = correlate(owner_rounds, channel_counts, group.reshape(1), waves, a, rn, tpb, slots, groups)
    out = pieces[0]
    for k in range(1, groups):
        out = out + lax.ppermute(pieces[k], "tmpl", [(i, (i + k) % groups) for i in range(groups)])
    return out


def solution(mesh):
    in_specs = (P(None, "tm"), P("tm", "tmpl", None), P(None, "tmpl"), P(), P())
    return jax.shard_map(shards, mesh=mesh, in_specs=in_specs, out_specs=P(None, ("tm", "tmpl")), check_vma=False)
```

```python
import functools

import jax
import jax.numpy as jnp
from jax import lax
from jax.experimental import pallas as pl
from jax.experimental.pallas import tpu as pltpu
from jax.sharding import PartitionSpec as P

bf16, f32, i32 = jnp.bfloat16, jnp.float32, jnp.int32
LANES = 128
FLOOR = 1e-6
GROUP = 8
UNROLL = 12
VMEM_LIMIT = 12 * 1024 * 1024


def in_hbm(x):
    return pltpu.with_memory_space_constraint(x, pltpu.HBM)


def vmem_spec():
    return pl.BlockSpec(memory_space=pltpu.VMEM)


def two_parts(x):
    hi = x.astype(bf16)
    return hi, (x - hi.astype(f32)).astype(bf16)


def chosen(owner, lists, tpb, t, s):
    return lists[s, owner[lax.div(t, tpb)] * tpb + lax.rem(t, tpb)]


def gather_kernel(tpb, owner, lists, wf, pairs, heads, scr, hs, sem):
    slots = lists.shape[0]
    n = pairs.shape[0]
    hb = heads.shape[0] // n

    def copy(i, c):
        pair = pl.multiple_of((c & 6), 2)
        return pltpu.make_async_copy(wf.at[c >> 3, :, pl.ds(pair, 2), :], pairs.at[i], sem.at[i])

    def start(t, _):
        def one(s, _):
            copy(t * slots + s, chosen(owner, lists, tpb, t, s)).start()
            return 0

        return lax.fori_loop(0, slots, one, 0, unroll=8)

    lax.fori_loop(0, n // slots, start, 0)

    def pick(t, _):
        def group(g, _):
            i = t * slots + g * GROUP
            for k in range(GROUP):
                copy(i + k, 0).wait()
            scr[0 : GROUP * 2 * hb, :] = pairs[pl.ds(i, GROUP), 0:hb].reshape(GROUP * 2 * hb, LANES).astype(f32)
            for k in range(GROUP):
                p = chosen(owner, lists, tpb, t, g * GROUP + k) & 1
                hs[pl.ds((i + k) * hb, hb), :] = scr[pl.ds(2 * hb * k + p, hb, stride=2), :]
            return 0

        return lax.fori_loop(0, slots // GROUP, group, 0)

    lax.fori_loop(0, n // slots, pick, 0)
    heads[...] = hs[...].astype(bf16)


def energy_kernel(tpb, taps, owner, lists, pairs, halo, rn, a, scr, band):
    slots = lists.shape[0]
    n, blocks = rn.shape[0], rn.shape[1]
    tb = taps // LANES
    half = blocks // 2
    l = lax.broadcasted_iota(i32, (LANES, LANES), 0)
    c = lax.broadcasted_iota(i32, (LANES, LANES), 1)
    before = jnp.where(l < c, 1.0, 0.0).astype(bf16)
    for k, piece in enumerate((jnp.ones_like(before), jnp.ones_like(before), before, before)):
        band[LANES * k : LANES * (k + 1), :] = piece

    def template(t, _):
        def group(g):
            base = t * slots + g * GROUP
            tails = halo[pl.ds(pl.multiple_of(base * tb, GROUP * tb), GROUP * tb), :].astype(f32)
            lhs = []
            for k in range(GROUP):
                i = base + k
                p = chosen(owner, lists, tpb, t, g * GROUP + k) & 1
                scr[g * GROUP + k, 0 : 2 * blocks, :] = pairs[i].astype(f32)
                scr[g * GROUP + k, pl.ds(2 * blocks + p, tb, stride=2), :] = tails[tb * k : tb * (k + 1)]
                q = []
                for v in range(tb + 2):
                    x = scr[g * GROUP + k, pl.ds(2 * v + p, half, stride=4), :]
                    a[i, half * v : half * (v + 1), :] = x.astype(bf16)
                    q.append(x * x)
                mid = functools.reduce(jnp.add, q[1:tb])
                for v in range(2):
                    whole, change = mid + q[v * tb], q[v + tb] - q[v]
                    lhs.append(jnp.concatenate(two_parts(whole) + two_parts(change), axis=1))
            e = jnp.dot(jnp.concatenate(lhs, axis=0), band[...], preferred_element_type=f32)
            e = lax.rsqrt(jnp.maximum(e, taps / 4.0))
            for k in range(GROUP):
                rn[base + k] = e[blocks * k : blocks * (k + 1)]

        for g in range(slots // GROUP):
            group(g)
        return 0

    lax.fori_loop(0, n // slots, template, 0)


def correlate_kernel(tpb, slots, owner, counts, place, w, a, rn, *refs):
    outs, (wr, scale, acc) = refs[:-3], refs[-3:]
    n, taps = w.shape
    tb = taps // LANES
    nt = n // slots
    blocks = rn.shape[1]
    half = blocks // 2
    parts = len(outs)
    group = place[0]
    wf = w[...].astype(f32)
    hi, lo = two_parts(wf * wf)
    ones = jnp.ones((taps, LANES), bf16)
    power = jnp.dot(hi, ones, preferred_element_type=f32) + jnp.dot(lo, ones, preferred_element_type=f32)
    norm = lax.rsqrt(power + FLOOR)
    slot_ids = lax.broadcasted_iota(i32, (slots, LANES), 0) + group * slots
    for t in range(nt):
        count = counts[owner[t // tpb] * tpb + t % tpb]
        scale[t * slots : (t + 1) * slots, :] = jnp.where(slot_ids < count, norm[t * slots : (t + 1) * slots], 0.0)
    row = lax.broadcasted_iota(i32, (LANES, LANES), 0)
    col = lax.broadcasted_iota(i32, (LANES, LANES), 1)
    flip = jnp.where(row + col == LANES - 1, 1.0, 0.0).astype(bf16)
    for j in range(tb):
        wr[j, 0:n, :] = jnp.dot(w[:, LANES * j : LANES * (j + 1)], flip, preferred_element_type=f32)
    own = row >= col
    zero = jnp.zeros((LANES, LANES), bf16)

    def one(i):
        d = [zero]
        for j in range(tb):
            b = jnp.concatenate([wr[j, pl.ds(i, 8, stride=0), :]] * (LANES // 8), axis=0)
            d.append(pltpu.roll(b, 1, axis=1, stride=1, stride_axis=0).astype(bf16))
        d.append(zero)
        band = jnp.concatenate([jnp.where(own, d[j + 1], d[j]) for j in range(tb + 1)], axis=0)
        x = jnp.concatenate([a[i, half * j : half * (j + 2), :] for j in range(tb + 1)], axis=1)
        out = jnp.dot(x, band, preferred_element_type=f32)
        s = scale[pl.ds(i, 8, stride=0), :]
        return out * rn[i] * jnp.concatenate([s] * (blocks // 8), axis=0)

    def template(t, _):
        r = lax.fori_loop(
            0, slots, lambda k, total: total + one(t * slots + k), jnp.zeros((blocks, LANES), f32), unroll=UNROLL
        )
        for v in range(2):
            acc[pl.ds(v * nt + t, half, stride=2 * nt), :] = r[half * v : half * (v + 1)]
        return 0

    lax.fori_loop(0, nt, template, 0)
    per = blocks // parts
    for k, o in enumerate(outs):
        to = (group + k) % parts
        for b in range(per):
            o[:, LANES * b : LANES * (b + 1)] = acc[pl.ds(pl.multiple_of((to * per + b) * nt, 8), nt), :]


def gather(owner, lists, wf4, tpb, tb):
    slots = lists.shape[0]
    n = owner.shape[0] * tpb * slots
    blocks = wf4.shape[1]
    return pl.pallas_call(
        functools.partial(gather_kernel, tpb),
        out_shape=(pltpu.VMEM((n, blocks, 2, LANES), bf16), jax.ShapeDtypeStruct((n * tb, LANES), bf16)),
        grid_spec=pltpu.PrefetchScalarGridSpec(
            num_scalar_prefetch=2,
            in_specs=[pl.BlockSpec(memory_space=pltpu.HBM)],
            out_specs=(vmem_spec(), vmem_spec()),
            scratch_shapes=[
                pltpu.VMEM((GROUP * 2 * tb + 8, LANES), f32),
                pltpu.VMEM((n * tb, LANES), f32),
                pltpu.SemaphoreType.DMA((n,)),
            ],
        ),
        compiler_params=pltpu.CompilerParams(vmem_limit_bytes=VMEM_LIMIT),
        name="gather_rows",
    )(in_hbm(owner), in_hbm(lists), in_hbm(wf4))


def energy(owner, lists, pairs, halo, tpb, taps):
    n, blocks = pairs.shape[0], pairs.shape[1] // 2
    tb = taps // LANES
    return pl.pallas_call(
        functools.partial(energy_kernel, tpb, taps),
        out_shape=(pltpu.VMEM((n, blocks, LANES), f32), pltpu.VMEM((n, blocks // 2 * (tb + 2), LANES), bf16)),
        grid_spec=pltpu.PrefetchScalarGridSpec(
            num_scalar_prefetch=2,
            in_specs=[vmem_spec(), vmem_spec()],
            out_specs=(vmem_spec(), vmem_spec()),
            scratch_shapes=[
                pltpu.VMEM((lists.shape[0], 2 * (blocks + tb) + 8, LANES), f32),
                pltpu.VMEM((4 * LANES, LANES), bf16),
            ],
        ),
        compiler_params=pltpu.CompilerParams(vmem_limit_bytes=VMEM_LIMIT),
        name="window_energy",
    )(in_hbm(owner), in_hbm(lists), pairs, halo)


def correlate(owner, counts, place, w, a, rn, tpb, slots, parts):
    n, taps = w.shape
    nt = n // slots
    blocks = rn.shape[1]
    return pl.pallas_call(
        functools.partial(correlate_kernel, tpb, slots),
        out_shape=tuple(jax.ShapeDtypeStruct((nt, blocks // parts * LANES), f32) for _ in range(parts)),
        grid_spec=pltpu.PrefetchScalarGridSpec(
            num_scalar_prefetch=3,
            in_specs=[vmem_spec()] * 3,
            out_specs=tuple(vmem_spec() for _ in range(parts)),
            scratch_shapes=[
                pltpu.VMEM((taps // LANES, n + 8, LANES), f32),
                pltpu.VMEM((n + 8, LANES), f32),
                pltpu.VMEM(((blocks + 2) * nt, LANES), f32),
            ],
        ),
        compiler_params=pltpu.CompilerParams(vmem_limit_bytes=VMEM_LIMIT),
        name="correlate",
    )(in_hbm(owner), in_hbm(counts), place, w, a, rn)


def turned(i, dy, dz):
    return ((i // 8 + dy) % 4) * 8 + ((i // 2 + dz) % 4) * 2 + i % 2


def sent(x, to):
    return lax.ppermute(x, "tm", [(i, to(i)) for i in range(32)])


def round_the_ring(x, first):
    total = x
    for k in (1, 3, 2):
        total = total + sent(x, lambda i: turned(i, 0, k) if (i % 2 == 0) == first else turned(i, k, 0))
    return total


def shards(waveforms, templates, channel_lists, channel_counts, owner_rounds):
    c, shard_len = waveforms.shape
    tpb, slots, taps = templates.shape
    rounds = owner_rounds.shape[0]
    n = rounds * tpb * slots
    me = lax.axis_index("tm")
    group = lax.axis_index("tmpl")
    groups = lax.axis_size("tmpl")
    wf4 = waveforms.reshape(c // 8, 8, shard_len // LANES, LANES).transpose(0, 2, 1, 3)
    other = sent(templates, lambda i: i ^ 1)
    owned = (owner_rounds == me)[:, None, None, None]
    paired = (owner_rounds == (me ^ 1))[:, None, None, None]
    nil = jnp.zeros((), templates.dtype)
    waves = jnp.where(owned, templates[None], jnp.where(paired, other[None], nil)).reshape(n, taps)
    waves = round_the_ring(waves, True)
    lists = channel_lists.T
    pairs, heads = gather(owner_rounds, lists, wf4, tpb, taps // LANES)
    pairs = pairs.reshape(n, -1, LANES)
    heads, waves = lax.optimization_barrier((heads, waves))
    halo = lax.ppermute(heads, "tm", [(i, i - 1) for i in range(1, 32)])
    waves = round_the_ring(waves, False)
    rn, a = energy(owner_rounds, lists, pairs, halo, tpb, taps)
    pieces = correlate(owner_rounds, channel_counts, group.reshape(1), waves, a, rn, tpb, slots, groups)
    out = pieces[0]
    for k in range(1, groups):
        out = out + lax.ppermute(pieces[k], "tmpl", [(i, (i + k) % groups) for i in range(groups)])
    return out


def solution(mesh):
    in_specs = (P(None, "tm"), P("tm", "tmpl", None), P(None, "tmpl"), P(), P())
    return jax.shard_map(shards, mesh=mesh, in_specs=in_specs, out_specs=P(None, ("tm", "tmpl")), check_vma=False)
```

```python
import functools

import jax
import jax.numpy as jnp
from jax import lax
from jax.experimental import pallas as pl
from jax.experimental.pallas import tpu as pltpu
from jax.sharding import PartitionSpec as P

bf16, f32, i32 = jnp.bfloat16, jnp.float32, jnp.int32
LANES = 128
FLOOR = 1e-6
GROUP = 8
UNROLL = 24
VMEM_LIMIT = 6 * 1024 * 1024


def in_hbm(x):
    return pltpu.with_memory_space_constraint(x, pltpu.HBM)


def vmem_spec():
    return pl.BlockSpec(memory_space=pltpu.VMEM)


def two_parts(x):
    hi = x.astype(bf16)
    return hi, (x - hi.astype(f32)).astype(bf16)


def template_id(owner, tpb, t):
    return owner[lax.div(t, tpb)] * tpb + lax.rem(t, tpb)


def gather_kernel(tpb, owner, lists, wf, pairs, heads, scr, hs, sem):
    slots = lists.shape[0]
    n = pairs.shape[0]
    hb = heads.shape[0] // n

    def copy(i, c):
        pair = pl.multiple_of(c & 6, 2)
        return pltpu.make_async_copy(wf.at[c >> 3, :, pl.ds(pair, 2), :], pairs.at[i], sem.at[i])

    def start(t, _):
        tid = template_id(owner, tpb, t)
        for s in range(slots):
            copy(t * slots + s, lists[s, tid]).start()
        return 0

    lax.fori_loop(0, n // slots, start, 0)

    def pick(t, _):
        tid = template_id(owner, tpb, t)
        for g in range(slots // GROUP):
            i = t * slots + g * GROUP
            for k in range(GROUP):
                copy(i + k, 0).wait()
            scr[g, 0 : GROUP * 2 * hb, :] = pairs[pl.ds(i, GROUP), 0:hb].reshape(GROUP * 2 * hb, LANES).astype(f32)
            for k in range(GROUP):
                p = lists[g * GROUP + k, tid] & 1
                hs[pl.ds((i + k) * hb, hb), :] = scr[g, pl.ds(2 * hb * k + p, hb, stride=2), :]
        return 0

    lax.fori_loop(0, n // slots, pick, 0)
    heads[...] = hs[...].astype(bf16)


def energy_kernel(tpb, taps, owner, lists, pairs, halo, rn, a, scr, band):
    slots = lists.shape[0]
    n, blocks = rn.shape[0], rn.shape[1]
    tb = taps // LANES
    half = blocks // 2
    l = lax.broadcasted_iota(i32, (LANES, LANES), 0)
    c = lax.broadcasted_iota(i32, (LANES, LANES), 1)
    before = jnp.where(l < c, 1.0, 0.0).astype(bf16)
    for k, piece in enumerate((jnp.ones_like(before), jnp.ones_like(before), before, before)):
        band[LANES * k : LANES * (k + 1), :] = piece

    def template(t, _):
        tid = template_id(owner, tpb, t)

        def group(g):
            base = t * slots + g * GROUP
            tails = halo[pl.ds(pl.multiple_of(base * tb, GROUP * tb), GROUP * tb), :].astype(f32)
            lhs = []
            for k in range(GROUP):
                i = base + k
                p = lists[g * GROUP + k, tid] & 1
                scr[g * GROUP + k, 0 : 2 * blocks, :] = pairs[i].astype(f32)
                scr[g * GROUP + k, pl.ds(2 * blocks + p, tb, stride=2), :] = tails[tb * k : tb * (k + 1)]
                q = []
                for v in range(tb + 2):
                    x = scr[g * GROUP + k, pl.ds(2 * v + p, half, stride=4), :]
                    a[i, half * v : half * (v + 1), :] = x.astype(bf16)
                    q.append(x * x)
                mid = functools.reduce(jnp.add, q[1:tb])
                for v in range(2):
                    whole, change = mid + q[v * tb], q[v + tb] - q[v]
                    lhs.append(jnp.concatenate(two_parts(whole) + two_parts(change), axis=1))
            e = jnp.dot(jnp.concatenate(lhs, axis=0), band[...], preferred_element_type=f32)
            e = lax.rsqrt(jnp.maximum(e, taps / 4.0))
            for k in range(GROUP):
                rn[base + k] = e[blocks * k : blocks * (k + 1)]

        for g in range(slots // GROUP):
            group(g)
        return 0

    lax.fori_loop(0, n // slots, template, 0)


def correlate_kernel(tpb, slots, owner, counts, place, w0, w1, w2, w3, a, rn, *refs):
    outs, (wr, scale, acc) = refs[:-3], refs[-3:]
    w = (w0[...] + w1[...]) + (w2[...] + w3[...])
    n, taps = w.shape
    tb = taps // LANES
    nt = n // slots
    blocks = rn.shape[1]
    half = blocks // 2
    parts = len(outs)
    group = place[0]
    wf = w.astype(f32)
    hi, lo = two_parts(wf * wf)
    ones = jnp.ones((taps, LANES), bf16)
    power = jnp.dot(hi, ones, preferred_element_type=f32) + jnp.dot(lo, ones, preferred_element_type=f32)
    norm = lax.rsqrt(power + FLOOR)
    slot_ids = lax.broadcasted_iota(i32, (slots, LANES), 0) + group * slots
    for t in range(nt):
        count = counts[owner[t // tpb] * tpb + t % tpb]
        scale[t * slots : (t + 1) * slots, :] = jnp.where(slot_ids < count, norm[t * slots : (t + 1) * slots], 0.0)
    row = lax.broadcasted_iota(i32, (LANES, LANES), 0)
    col = lax.broadcasted_iota(i32, (LANES, LANES), 1)
    flip = jnp.where(row + col == LANES - 1, 1.0, 0.0).astype(bf16)
    for j in range(tb):
        wr[j, 0:n, :] = jnp.dot(w[:, LANES * j : LANES * (j + 1)], flip, preferred_element_type=f32)
    own = row >= col
    zero = jnp.zeros((LANES, LANES), bf16)

    def one(i):
        d = [zero]
        for j in range(tb):
            b = jnp.concatenate([wr[j, pl.ds(i, 8, stride=0), :]] * (LANES // 8), axis=0)
            d.append(pltpu.roll(b, 1, axis=1, stride=1, stride_axis=0).astype(bf16))
        d.append(zero)
        band = jnp.concatenate([jnp.where(own, d[j + 1], d[j]) for j in range(tb + 1)], axis=0)
        x = jnp.concatenate([a[i, half * j : half * (j + 2), :] for j in range(tb + 1)], axis=1)
        out = jnp.dot(x, band, preferred_element_type=f32)
        s = scale[pl.ds(i, 8, stride=0), :]
        return out * rn[i] * jnp.concatenate([s] * (blocks // 8), axis=0)

    def template(t, _):
        r = lax.fori_loop(
            0, slots, lambda k, total: total + one(t * slots + k), jnp.zeros((blocks, LANES), f32), unroll=UNROLL
        )
        for v in range(2):
            acc[pl.ds(v * nt + t, half, stride=2 * nt), :] = r[half * v : half * (v + 1)]
        return 0

    lax.fori_loop(0, nt, template, 0)
    per = blocks // parts
    for k, o in enumerate(outs):
        to = (group + k) % parts
        for b in range(per):
            o[:, LANES * b : LANES * (b + 1)] = acc[pl.ds(pl.multiple_of((to * per + b) * nt, 8), nt), :]


def gather(owner, lists, wf4, tpb, tb):
    slots = lists.shape[0]
    n = owner.shape[0] * tpb * slots
    blocks = wf4.shape[1]
    return pl.pallas_call(
        functools.partial(gather_kernel, tpb),
        out_shape=(pltpu.VMEM((n, blocks, 2, LANES), bf16), jax.ShapeDtypeStruct((n * tb, LANES), bf16)),
        grid_spec=pltpu.PrefetchScalarGridSpec(
            num_scalar_prefetch=2,
            in_specs=[pl.BlockSpec(memory_space=pltpu.HBM)],
            out_specs=(vmem_spec(), vmem_spec()),
            scratch_shapes=[
                pltpu.VMEM((slots // GROUP, GROUP * 2 * tb + 8, LANES), f32),
                pltpu.VMEM((n * tb, LANES), f32),
                pltpu.SemaphoreType.DMA((n,)),
            ],
        ),
        compiler_params=pltpu.CompilerParams(vmem_limit_bytes=VMEM_LIMIT),
        name="gather_rows",
    )(in_hbm(owner), in_hbm(lists), in_hbm(wf4))


def energy(owner, lists, pairs, halo, tpb, taps):
    n, blocks = pairs.shape[0], pairs.shape[1] // 2
    tb = taps // LANES
    return pl.pallas_call(
        functools.partial(energy_kernel, tpb, taps),
        out_shape=(pltpu.VMEM((n, blocks, LANES), f32), pltpu.VMEM((n, blocks // 2 * (tb + 2), LANES), bf16)),
        grid_spec=pltpu.PrefetchScalarGridSpec(
            num_scalar_prefetch=2,
            in_specs=[vmem_spec(), vmem_spec()],
            out_specs=(vmem_spec(), vmem_spec()),
            scratch_shapes=[
                pltpu.VMEM((lists.shape[0], 2 * (blocks + tb) + 8, LANES), f32),
                pltpu.VMEM((4 * LANES, LANES), bf16),
            ],
        ),
        compiler_params=pltpu.CompilerParams(vmem_limit_bytes=VMEM_LIMIT),
        name="window_energy",
    )(in_hbm(owner), in_hbm(lists), pairs, halo)


def correlate(owner, counts, place, ws, a, rn, tpb, slots, parts):
    n, taps = ws[0].shape
    nt = n // slots
    blocks = rn.shape[1]
    return pl.pallas_call(
        functools.partial(correlate_kernel, tpb, slots),
        out_shape=tuple(jax.ShapeDtypeStruct((nt, blocks // parts * LANES), f32) for _ in range(parts)),
        grid_spec=pltpu.PrefetchScalarGridSpec(
            num_scalar_prefetch=3,
            in_specs=[vmem_spec()] * (len(ws) + 2),
            out_specs=tuple(vmem_spec() for _ in range(parts)),
            scratch_shapes=[
                pltpu.VMEM((taps // LANES, n + 8, LANES), f32),
                pltpu.VMEM((n + 8, LANES), f32),
                pltpu.VMEM(((blocks + 2) * nt, LANES), f32),
            ],
        ),
        compiler_params=pltpu.CompilerParams(vmem_limit_bytes=VMEM_LIMIT),
        name="correlate",
    )(in_hbm(owner), in_hbm(counts), place, *ws, a, rn)


def turned(i, dy, dz):
    return ((i // 8 + dy) % 4) * 8 + ((i // 2 + dz) % 4) * 2 + i % 2


def sent(x, to):
    return lax.ppermute(x, "tm", [(i, to(i)) for i in range(32)])


def round_the_ring(x, first):
    turn = lambda k: lambda i: turned(i, 0, k) if (i % 2 == 0) == first else turned(i, k, 0)
    return [x] + [sent(x, turn(k)) for k in (1, 3, 2)]


def shards(waveforms, templates, channel_lists, channel_counts, owner_rounds):
    c, shard_len = waveforms.shape
    tpb, slots, taps = templates.shape
    rounds = owner_rounds.shape[0]
    n = rounds * tpb * slots
    me = lax.axis_index("tm")
    group = lax.axis_index("tmpl")
    groups = lax.axis_size("tmpl")
    wf4 = waveforms.reshape(c // 8, 8, shard_len // LANES, LANES).transpose(0, 2, 1, 3)
    other = sent(templates, lambda i: i ^ 1)
    owned = (owner_rounds == me)[:, None, None, None]
    paired = (owner_rounds == (me ^ 1))[:, None, None, None]
    nil = jnp.zeros((), templates.dtype)
    waves = jnp.where(owned, templates[None], jnp.where(paired, other[None], nil)).reshape(n, taps)
    waves = functools.reduce(jnp.add, round_the_ring(waves, True))
    lists = channel_lists.T
    pairs, heads = gather(owner_rounds, lists, wf4, tpb, taps // LANES)
    pairs = pairs.reshape(n, -1, LANES)
    heads, waves = lax.optimization_barrier((heads, waves))
    halo = lax.ppermute(heads, "tm", [(i, i - 1) for i in range(1, 32)])
    waves = round_the_ring(waves, False)
    rn, a = energy(owner_rounds, lists, pairs, halo, tpb, taps)
    pieces = correlate(owner_rounds, channel_counts, group.reshape(1), waves, a, rn, tpb, slots, groups)
    out = pieces[0]
    for k in range(1, groups):
        out = out + lax.ppermute(pieces[k], "tmpl", [(i, (i + k) % groups) for i in range(groups)])
    return out


def solution(mesh):
    in_specs = (P(None, "tm"), P("tm", "tmpl", None), P(None, "tmpl"), P(), P())
    return jax.shard_map(shards, mesh=mesh, in_specs=in_specs, out_specs=P(None, ("tm", "tmpl")), check_vma=False)
```

```python
import functools

import jax
import jax.numpy as jnp
from jax import lax
from jax.experimental import pallas as pl
from jax.experimental.pallas import tpu as pltpu
from jax.sharding import PartitionSpec as P

bf16, f32, i32 = jnp.bfloat16, jnp.float32, jnp.int32
LANES = 128
FLOOR = 1e-6
GROUP = 8
UNROLL = 24
EACH = 2
VMEM_LIMIT = 6 * 1024 * 1024


def in_hbm(x):
    return pltpu.with_memory_space_constraint(x, pltpu.HBM)


def vmem_spec():
    return pl.BlockSpec(memory_space=pltpu.VMEM)


def two_parts(x):
    hi = x.astype(bf16)
    return hi, (x - hi.astype(f32)).astype(bf16)


def template_id(owner, tpb, t):
    return owner[lax.div(t, tpb)] * tpb + lax.rem(t, tpb)


def gather_kernel(tpb, owner, lists, wf, pairs, heads, scr, hs, sem):
    slots = lists.shape[0]
    n = pairs.shape[0]
    hb = heads.shape[0] // n

    def copy(i, c):
        pair = pl.multiple_of(c & 6, 2)
        return pltpu.make_async_copy(wf.at[c >> 3, :, pl.ds(pair, 2), :], pairs.at[i], sem.at[i])

    def start(t, _):
        tid = template_id(owner, tpb, t)
        for s in range(slots):
            copy(t * slots + s, lists[s, tid]).start()
        return 0

    lax.fori_loop(0, n // slots, start, 0)

    def pick(t, _):
        tid = template_id(owner, tpb, t)
        for g in range(slots // GROUP):
            i = t * slots + g * GROUP
            for k in range(GROUP):
                copy(i + k, 0).wait()
            scr[g, 0 : GROUP * 2 * hb, :] = pairs[pl.ds(i, GROUP), 0:hb].reshape(GROUP * 2 * hb, LANES).astype(f32)
            for k in range(GROUP):
                p = lists[g * GROUP + k, tid] & 1
                hs[pl.ds((i + k) * hb, hb), :] = scr[g, pl.ds(2 * hb * k + p, hb, stride=2), :]
        return 0

    lax.fori_loop(0, n // slots, pick, 0)
    heads[...] = hs[...].astype(bf16)


def energy_kernel(tpb, taps, owner, lists, pairs, halo, rn, a, scr, band):
    slots = lists.shape[0]
    n, blocks = rn.shape[0], rn.shape[1]
    tb = taps // LANES
    half = blocks // 2
    l = lax.broadcasted_iota(i32, (LANES, LANES), 0)
    c = lax.broadcasted_iota(i32, (LANES, LANES), 1)
    before = jnp.where(l < c, 1.0, 0.0).astype(bf16)
    for k, piece in enumerate((jnp.ones_like(before), jnp.ones_like(before), before, before)):
        band[LANES * k : LANES * (k + 1), :] = piece

    def template(t, at):
        tid = template_id(owner, tpb, t)

        def group(g):
            base = t * slots + g * GROUP
            tails = halo[pl.ds(pl.multiple_of(base * tb, GROUP * tb), GROUP * tb), :].astype(f32)
            lhs = []
            for k in range(GROUP):
                i = base + k
                p = lists[g * GROUP + k, tid] & 1
                scr[at * slots + g * GROUP + k, 0 : 2 * blocks, :] = pairs[i].astype(f32)
                scr[at * slots + g * GROUP + k, pl.ds(2 * blocks + p, tb, stride=2), :] = tails[tb * k : tb * (k + 1)]
                q = []
                for v in range(tb + 2):
                    x = scr[at * slots + g * GROUP + k, pl.ds(2 * v + p, half, stride=4), :]
                    a[i, half * v : half * (v + 1), :] = x.astype(bf16)
                    q.append(x * x)
                mid = functools.reduce(jnp.add, q[1:tb])
                for v in range(2):
                    whole, change = mid + q[v * tb], q[v + tb] - q[v]
                    lhs.append(jnp.concatenate(two_parts(whole) + two_parts(change), axis=1))
            e = jnp.dot(jnp.concatenate(lhs, axis=0), band[...], preferred_element_type=f32)
            e = lax.rsqrt(jnp.maximum(e, taps / 4.0))
            for k in range(GROUP):
                rn[base + k] = e[blocks * k : blocks * (k + 1)]

        for g in range(slots // GROUP):
            group(g)

    def step(u, _):
        for at in range(EACH):
            template(u * EACH + at, at)
        return 0

    lax.fori_loop(0, n // slots // EACH, step, 0)


def correlate_kernel(tpb, slots, owner, counts, place, w0, w1, w2, w3, a, rn, *refs):
    outs, (wr, scale, acc) = refs[:-3], refs[-3:]
    w = (w0[...] + w1[...]) + (w2[...] + w3[...])
    n, taps = w.shape
    tb = taps // LANES
    nt = n // slots
    blocks = rn.shape[1]
    half = blocks // 2
    parts = len(outs)
    group = place[0]
    wf = w.astype(f32)
    hi, lo = two_parts(wf * wf)
    ones = jnp.ones((taps, LANES), bf16)
    power = jnp.dot(hi, ones, preferred_element_type=f32) + jnp.dot(lo, ones, preferred_element_type=f32)
    norm = lax.rsqrt(power + FLOOR)
    slot_ids = lax.broadcasted_iota(i32, (slots, LANES), 0) + group * slots
    for t in range(nt):
        count = counts[owner[t // tpb] * tpb + t % tpb]
        scale[t * slots : (t + 1) * slots, :] = jnp.where(slot_ids < count, norm[t * slots : (t + 1) * slots], 0.0)
    row = lax.broadcasted_iota(i32, (LANES, LANES), 0)
    col = lax.broadcasted_iota(i32, (LANES, LANES), 1)
    flip = jnp.where(row + col == LANES - 1, 1.0, 0.0).astype(bf16)
    for j in range(tb):
        wr[j, 0:n, :] = jnp.dot(w[:, LANES * j : LANES * (j + 1)], flip, preferred_element_type=f32)
    own = row >= col
    zero = jnp.zeros((LANES, LANES), bf16)

    def one(i):
        d = [zero]
        for j in range(tb):
            b = jnp.concatenate([wr[j, pl.ds(i, 8, stride=0), :]] * (LANES // 8), axis=0)
            d.append(pltpu.roll(b, 1, axis=1, stride=1, stride_axis=0).astype(bf16))
        d.append(zero)
        band = jnp.concatenate([jnp.where(own, d[j + 1], d[j]) for j in range(tb + 1)], axis=0)
        x = jnp.concatenate([a[i, half * j : half * (j + 2), :] for j in range(tb + 1)], axis=1)
        out = jnp.dot(x, band, preferred_element_type=f32)
        s = scale[pl.ds(i, 8, stride=0), :]
        return out * rn[i] * jnp.concatenate([s] * (blocks // 8), axis=0)

    def template(t, _):
        r = lax.fori_loop(
            0, slots, lambda k, total: total + one(t * slots + k), jnp.zeros((blocks, LANES), f32), unroll=UNROLL
        )
        for v in range(2):
            acc[pl.ds(v * nt + t, half, stride=2 * nt), :] = r[half * v : half * (v + 1)]
        return 0

    lax.fori_loop(0, nt, template, 0)
    per = blocks // parts
    for k, o in enumerate(outs):
        to = (group + k) % parts
        for b in range(per):
            o[:, LANES * b : LANES * (b + 1)] = acc[pl.ds(pl.multiple_of((to * per + b) * nt, 8), nt), :]


def gather(owner, lists, wf4, tpb, tb):
    slots = lists.shape[0]
    n = owner.shape[0] * tpb * slots
    blocks = wf4.shape[1]
    return pl.pallas_call(
        functools.partial(gather_kernel, tpb),
        out_shape=(pltpu.VMEM((n, blocks, 2, LANES), bf16), jax.ShapeDtypeStruct((n * tb, LANES), bf16)),
        grid_spec=pltpu.PrefetchScalarGridSpec(
            num_scalar_prefetch=2,
            in_specs=[pl.BlockSpec(memory_space=pltpu.HBM)],
            out_specs=(vmem_spec(), vmem_spec()),
            scratch_shapes=[
                pltpu.VMEM((slots // GROUP, GROUP * 2 * tb + 8, LANES), f32),
                pltpu.VMEM((n * tb, LANES), f32),
                pltpu.SemaphoreType.DMA((n,)),
            ],
        ),
        compiler_params=pltpu.CompilerParams(vmem_limit_bytes=VMEM_LIMIT),
        name="gather_rows",
    )(in_hbm(owner), in_hbm(lists), in_hbm(wf4))


def energy(owner, lists, pairs, halo, tpb, taps):
    n, blocks = pairs.shape[0], pairs.shape[1] // 2
    tb = taps // LANES
    return pl.pallas_call(
        functools.partial(energy_kernel, tpb, taps),
        out_shape=(pltpu.VMEM((n, blocks, LANES), f32), pltpu.VMEM((n, blocks // 2 * (tb + 2), LANES), bf16)),
        grid_spec=pltpu.PrefetchScalarGridSpec(
            num_scalar_prefetch=2,
            in_specs=[vmem_spec(), vmem_spec()],
            out_specs=(vmem_spec(), vmem_spec()),
            scratch_shapes=[
                pltpu.VMEM((EACH * lists.shape[0], 2 * (blocks + tb) + 8, LANES), f32),
                pltpu.VMEM((4 * LANES, LANES), bf16),
            ],
        ),
        compiler_params=pltpu.CompilerParams(vmem_limit_bytes=VMEM_LIMIT),
        name="window_energy",
    )(in_hbm(owner), in_hbm(lists), pairs, halo)


def correlate(owner, counts, place, ws, a, rn, tpb, slots, parts):
    n, taps = ws[0].shape
    nt = n // slots
    blocks = rn.shape[1]
    return pl.pallas_call(
        functools.partial(correlate_kernel, tpb, slots),
        out_shape=tuple(jax.ShapeDtypeStruct((nt, blocks // parts * LANES), f32) for _ in range(parts)),
        grid_spec=pltpu.PrefetchScalarGridSpec(
            num_scalar_prefetch=3,
            in_specs=[vmem_spec()] * (len(ws) + 2),
            out_specs=tuple(vmem_spec() for _ in range(parts)),
            scratch_shapes=[
                pltpu.VMEM((taps // LANES, n + 8, LANES), f32),
                pltpu.VMEM((n + 8, LANES), f32),
                pltpu.VMEM(((blocks + 2) * nt, LANES), f32),
            ],
        ),
        compiler_params=pltpu.CompilerParams(vmem_limit_bytes=VMEM_LIMIT),
        name="correlate",
    )(in_hbm(owner), in_hbm(counts), place, *ws, a, rn)


def turned(i, dy, dz):
    return ((i // 8 + dy) % 4) * 8 + ((i // 2 + dz) % 4) * 2 + i % 2


def sent(x, to):
    return lax.ppermute(x, "tm", [(i, to(i)) for i in range(32)])


def round_the_ring(x, first):
    turn = lambda k: lambda i: turned(i, 0, k) if (i % 2 == 0) == first else turned(i, k, 0)
    return [x] + [sent(x, turn(k)) for k in (1, 3, 2)]


def shards(waveforms, templates, channel_lists, channel_counts, owner_rounds):
    c, shard_len = waveforms.shape
    tpb, slots, taps = templates.shape
    rounds = owner_rounds.shape[0]
    n = rounds * tpb * slots
    me = lax.axis_index("tm")
    group = lax.axis_index("tmpl")
    groups = lax.axis_size("tmpl")
    wf4 = waveforms.reshape(c // 8, 8, shard_len // LANES, LANES).transpose(0, 2, 1, 3)
    other = sent(templates, lambda i: i ^ 1)
    owned = (owner_rounds == me)[:, None, None, None]
    paired = (owner_rounds == (me ^ 1))[:, None, None, None]
    nil = jnp.zeros((), templates.dtype)
    waves = jnp.where(owned, templates[None], jnp.where(paired, other[None], nil)).reshape(n, taps)
    waves = functools.reduce(jnp.add, round_the_ring(waves, True))
    lists = channel_lists.T
    pairs, heads = gather(owner_rounds, lists, wf4, tpb, taps // LANES)
    pairs = pairs.reshape(n, -1, LANES)
    heads, waves = lax.optimization_barrier((heads, waves))
    halo = lax.ppermute(heads, "tm", [(i, i - 1) for i in range(1, 32)])
    waves = round_the_ring(waves, False)
    rn, a = energy(owner_rounds, lists, pairs, halo, tpb, taps)
    pieces = list(
        correlate(owner_rounds, channel_counts, group.reshape(1), waves, a, rn, tpb, slots, groups)
    )
    for k in range(1, groups):
        pieces[k] = lax.ppermute(pieces[k], "tmpl", [(i, (i + k) % groups) for i in range(groups)])
    return (pieces[0] + pieces[1]) + (pieces[2] + pieces[3])


def solution(mesh):
    in_specs = (P(None, "tm"), P("tm", "tmpl", None), P(None, "tmpl"), P(), P())
    return jax.shard_map(shards, mesh=mesh, in_specs=in_specs, out_specs=P(None, ("tm", "tmpl")), check_vma=False)
```

```python
import functools

import jax
import jax.numpy as jnp
from jax import lax
from jax.experimental import pallas as pl
from jax.experimental.pallas import tpu as pltpu
from jax.sharding import PartitionSpec as P

bf16, f32, i32 = jnp.bfloat16, jnp.float32, jnp.int32
LANES = 128
FLOOR = 1e-6
GROUP = 8
UNROLL = 24
EACH = 2
VMEM_LIMIT = 6 * 1024 * 1024


def in_hbm(x):
    return pltpu.with_memory_space_constraint(x, pltpu.HBM)


def vmem_spec():
    return pl.BlockSpec(memory_space=pltpu.VMEM)


def two_parts(x):
    hi = x.astype(bf16)
    return hi, (x - hi.astype(f32)).astype(bf16)


def template_id(owner, tpb, t):
    return owner[lax.div(t, tpb)] * tpb + lax.rem(t, tpb)


def gather_kernel(tpb, owner, lists, wf, pairs, heads, scr, hs, sem):
    slots = lists.shape[0]
    n = pairs.shape[0]
    hb = heads.shape[0] // n

    def copy(i, c):
        pair = pl.multiple_of(c & 6, 2)
        return pltpu.make_async_copy(wf.at[c >> 3, :, pl.ds(pair, 2), :], pairs.at[i], sem.at[i])

    def start(t, _):
        tid = template_id(owner, tpb, t)
        for s in range(slots):
            copy(t * slots + s, lists[s, tid]).start()
        return 0

    lax.fori_loop(0, n // slots, start, 0)

    def pick(t, _):
        tid = template_id(owner, tpb, t)
        for g in range(slots // GROUP):
            i = t * slots + g * GROUP
            for k in range(GROUP):
                copy(i + k, 0).wait()
            scr[g, 0 : GROUP * 2 * hb, :] = pairs[pl.ds(i, GROUP), 0:hb].reshape(GROUP * 2 * hb, LANES).astype(f32)
            for k in range(GROUP):
                p = lists[g * GROUP + k, tid] & 1
                hs[pl.ds((i + k) * hb, hb), :] = scr[g, pl.ds(2 * hb * k + p, hb, stride=2), :]
        return 0

    lax.fori_loop(0, n // slots, pick, 0)
    heads[...] = hs[...].astype(bf16)


def energy_kernel(tpb, taps, owner, lists, pairs, halo, rn, a, scr, band):
    slots = lists.shape[0]
    n, blocks = rn.shape[0], rn.shape[1]
    tb = taps // LANES
    half = blocks // 2
    l = lax.broadcasted_iota(i32, (LANES, LANES), 0)
    c = lax.broadcasted_iota(i32, (LANES, LANES), 1)
    before = jnp.where(l < c, 1.0, 0.0).astype(bf16)
    for k, piece in enumerate((jnp.ones_like(before), jnp.ones_like(before), before, before)):
        band[LANES * k : LANES * (k + 1), :] = piece

    def template(t, at):
        tid = template_id(owner, tpb, t)

        def group(g):
            base = t * slots + g * GROUP
            tails = halo[pl.ds(pl.multiple_of(base * tb, GROUP * tb), GROUP * tb), :].astype(f32)
            lhs = []
            for k in range(GROUP):
                i = base + k
                p = lists[g * GROUP + k, tid] & 1
                scr[at * slots + g * GROUP + k, 0 : 2 * blocks, :] = pairs[i].astype(f32)
                scr[at * slots + g * GROUP + k, pl.ds(2 * blocks + p, tb, stride=2), :] = tails[tb * k : tb * (k + 1)]
                q = []
                for v in range(tb + 2):
                    x = scr[at * slots + g * GROUP + k, pl.ds(2 * v + p, half, stride=4), :]
                    a[i, half * v : half * (v + 1), :] = x.astype(bf16)
                    q.append(x * x)
                mid = functools.reduce(jnp.add, q[1:tb])
                for v in range(2):
                    whole, change = mid + q[v * tb], q[v + tb] - q[v]
                    lhs.append(jnp.concatenate(two_parts(whole) + two_parts(change), axis=1))
            e = jnp.dot(jnp.concatenate(lhs, axis=0), band[...], preferred_element_type=f32)
            e = lax.rsqrt(jnp.maximum(e, taps / 4.0))
            for k in range(GROUP):
                rn[base + k] = e[blocks * k : blocks * (k + 1)]

        for g in range(slots // GROUP):
            group(g)

    def step(u, _):
        for at in range(EACH):
            template(u * EACH + at, at)
        return 0

    lax.fori_loop(0, n // slots // EACH, step, 0)


def correlate_kernel(tpb, slots, owner, counts, place, w0, w1, w2, w3, a, rn, *refs):
    outs, (wr, scale, acc) = refs[:-3], refs[-3:]
    w = (w0[...] + w1[...]) + (w2[...] + w3[...])
    n, taps = w.shape
    tb = taps // LANES
    nt = n // slots
    blocks = rn.shape[1]
    half = blocks // 2
    parts = 4
    group = place[0]
    wf = w.astype(f32)
    hi, lo = two_parts(wf * wf)
    ones = jnp.ones((taps, LANES), bf16)
    power = jnp.dot(hi, ones, preferred_element_type=f32) + jnp.dot(lo, ones, preferred_element_type=f32)
    norm = lax.rsqrt(power + FLOOR)
    slot_ids = lax.broadcasted_iota(i32, (slots, LANES), 0) + group * slots
    for t in range(nt):
        count = counts[owner[t // tpb] * tpb + t % tpb]
        scale[t * slots : (t + 1) * slots, :] = jnp.where(slot_ids < count, norm[t * slots : (t + 1) * slots], 0.0)
    row = lax.broadcasted_iota(i32, (LANES, LANES), 0)
    col = lax.broadcasted_iota(i32, (LANES, LANES), 1)
    flip = jnp.where(row + col == LANES - 1, 1.0, 0.0).astype(bf16)
    for j in range(tb):
        wr[j, 0:n, :] = jnp.dot(w[:, LANES * j : LANES * (j + 1)], flip, preferred_element_type=f32)
    own = row >= col
    zero = jnp.zeros((LANES, LANES), bf16)

    def one(i):
        d = [zero]
        for j in range(tb):
            b = jnp.concatenate([wr[j, pl.ds(i, 8, stride=0), :]] * (LANES // 8), axis=0)
            d.append(pltpu.roll(b, 1, axis=1, stride=1, stride_axis=0).astype(bf16))
        d.append(zero)
        band = jnp.concatenate([jnp.where(own, d[j + 1], d[j]) for j in range(tb + 1)], axis=0)
        x = jnp.concatenate([a[i, half * j : half * (j + 2), :] for j in range(tb + 1)], axis=1)
        out = jnp.dot(x, band, preferred_element_type=f32)
        s = scale[pl.ds(i, 8, stride=0), :]
        return out * rn[i] * jnp.concatenate([s] * (blocks // 8), axis=0)

    def template(t, _):
        r = lax.fori_loop(
            0, slots, lambda k, total: total + one(t * slots + k), jnp.zeros((blocks, LANES), f32), unroll=UNROLL
        )
        for v in range(2):
            acc[pl.ds(v * nt + t, half, stride=2 * nt), :] = r[half * v : half * (v + 1)]
        return 0

    lax.fori_loop(0, nt, template, 0)
    per = blocks // parts
    aside = group ^ 1
    last = parts - 1
    for o, row, to in (
        (outs[0], 0, group),
        (outs[1], 0, last - group),
        (outs[2], 0, last - aside),
        (outs[2], nt, aside),
    ):
        for b in range(per):
            piece = acc[pl.ds(pl.multiple_of((to * per + b) * nt, 8), nt), :]
            o[row : row + nt, LANES * b : LANES * (b + 1)] = piece


def gather(owner, lists, wf4, tpb, tb):
    slots = lists.shape[0]
    n = owner.shape[0] * tpb * slots
    blocks = wf4.shape[1]
    return pl.pallas_call(
        functools.partial(gather_kernel, tpb),
        out_shape=(pltpu.VMEM((n, blocks, 2, LANES), bf16), pltpu.VMEM((n * tb, LANES), bf16)),
        grid_spec=pltpu.PrefetchScalarGridSpec(
            num_scalar_prefetch=2,
            in_specs=[pl.BlockSpec(memory_space=pltpu.HBM)],
            out_specs=(vmem_spec(), vmem_spec()),
            scratch_shapes=[
                pltpu.VMEM((slots // GROUP, GROUP * 2 * tb + 8, LANES), f32),
                pltpu.VMEM((n * tb, LANES), f32),
                pltpu.SemaphoreType.DMA((n,)),
            ],
        ),
        compiler_params=pltpu.CompilerParams(vmem_limit_bytes=VMEM_LIMIT),
        name="gather_rows",
    )(in_hbm(owner), in_hbm(lists), in_hbm(wf4))


def energy(owner, lists, pairs, halo, tpb, taps):
    n, blocks = pairs.shape[0], pairs.shape[1] // 2
    tb = taps // LANES
    return pl.pallas_call(
        functools.partial(energy_kernel, tpb, taps),
        out_shape=(pltpu.VMEM((n, blocks, LANES), f32), pltpu.VMEM((n, blocks // 2 * (tb + 2), LANES), bf16)),
        grid_spec=pltpu.PrefetchScalarGridSpec(
            num_scalar_prefetch=2,
            in_specs=[vmem_spec(), vmem_spec()],
            out_specs=(vmem_spec(), vmem_spec()),
            scratch_shapes=[
                pltpu.VMEM((EACH * lists.shape[0], 2 * (blocks + tb) + 8, LANES), f32),
                pltpu.VMEM((4 * LANES, LANES), bf16),
            ],
        ),
        compiler_params=pltpu.CompilerParams(vmem_limit_bytes=VMEM_LIMIT),
        name="window_energy",
    )(in_hbm(owner), in_hbm(lists), pairs, halo)


def correlate(owner, counts, place, ws, a, rn, tpb, slots, parts):
    n, taps = ws[0].shape
    nt = n // slots
    blocks = rn.shape[1]
    return pl.pallas_call(
        functools.partial(correlate_kernel, tpb, slots),
        out_shape=tuple(jax.ShapeDtypeStruct((r * nt, blocks // parts * LANES), f32) for r in (1, 1, 2)),
        grid_spec=pltpu.PrefetchScalarGridSpec(
            num_scalar_prefetch=3,
            in_specs=[vmem_spec()] * (len(ws) + 2),
            out_specs=tuple(vmem_spec() for _ in range(3)),
            scratch_shapes=[
                pltpu.VMEM((taps // LANES, n + 8, LANES), f32),
                pltpu.VMEM((n + 8, LANES), f32),
                pltpu.VMEM(((blocks + 2) * nt, LANES), f32),
            ],
        ),
        compiler_params=pltpu.CompilerParams(vmem_limit_bytes=VMEM_LIMIT),
        name="correlate",
    )(in_hbm(owner), in_hbm(counts), place, *ws, a, rn)


def turned(i, dy, dz):
    return ((i // 8 + dy) % 4) * 8 + ((i // 2 + dz) % 4) * 2 + i % 2


def sent(x, to):
    return lax.ppermute(x, "tm", [(i, to(i)) for i in range(32)])


def round_the_ring(x, first):
    turn = lambda k: lambda i: turned(i, 0, k) if (i % 2 == 0) == first else turned(i, k, 0)
    return [x] + [sent(x, turn(k)) for k in (1, 3, 2)]


def shards(waveforms, templates, channel_lists, channel_counts, owner_rounds):
    c, shard_len = waveforms.shape
    tpb, slots, taps = templates.shape
    rounds = owner_rounds.shape[0]
    n = rounds * tpb * slots
    me = lax.axis_index("tm")
    group = lax.axis_index("tmpl")
    groups = lax.axis_size("tmpl")
    wf4 = waveforms.reshape(c // 8, 8, shard_len // LANES, LANES).transpose(0, 2, 1, 3)
    other = sent(templates, lambda i: i ^ 1)
    owned = (owner_rounds == me)[:, None, None, None]
    paired = (owner_rounds == (me ^ 1))[:, None, None, None]
    nil = jnp.zeros((), templates.dtype)
    waves = jnp.where(owned, templates[None], jnp.where(paired, other[None], nil)).reshape(n, taps)
    waves = functools.reduce(jnp.add, round_the_ring(waves, True))
    lists = channel_lists.T
    pairs, heads = gather(owner_rounds, lists, wf4, tpb, taps // LANES)
    pairs = pairs.reshape(n, -1, LANES)
    heads, waves = lax.optimization_barrier((heads, waves))
    halo = lax.ppermute(heads, "tm", [(i, i - 1) for i in range(1, 32)])
    waves = round_the_ring(waves, False)
    rn, a = energy(owner_rounds, lists, pairs, halo, tpb, taps)
    nt = rounds * tpb
    mine, later, given = correlate(
        owner_rounds, channel_counts, group.reshape(1), waves, a, rn, tpb, slots, groups
    )
    taken = lax.ppermute(given, "tmpl", [(i, i ^ 1) for i in range(groups)])
    share = lax.ppermute(later + taken[0:nt], "tmpl", [(i, groups - 1 - i) for i in range(groups)])
    return mine + taken[nt:] + share


def solution(mesh):
    in_specs = (P(None, "tm"), P("tm", "tmpl", None), P(None, "tmpl"), P(), P())
    return jax.shard_map(shards, mesh=mesh, in_specs=in_specs, out_specs=P(None, ("tm", "tmpl")), check_vma=False)
```

```python
import functools

import jax
import jax.numpy as jnp
from jax import lax
from jax.experimental import pallas as pl
from jax.experimental.pallas import tpu as pltpu
from jax.sharding import PartitionSpec as P

bf16, f32, i32 = jnp.bfloat16, jnp.float32, jnp.int32
LANES = 128
FLOOR = 1e-6
GROUP = 8
UNROLL = 24
EACH = 2
VMEM_LIMIT = 6 * 1024 * 1024


def in_hbm(x):
    return pltpu.with_memory_space_constraint(x, pltpu.HBM)


def vmem_spec():
    return pl.BlockSpec(memory_space=pltpu.VMEM)


def two_parts(x):
    hi = x.astype(bf16)
    return hi, (x - hi.astype(f32)).astype(bf16)


def template_id(owner, tpb, t):
    return owner[lax.div(t, tpb)] * tpb + lax.rem(t, tpb)


def gather_kernel(tpb, owner, lists, wf, pairs, heads, scr, hs, sem):
    slots = lists.shape[0]
    n = pairs.shape[0]
    hb = heads.shape[0] // n

    def copy(i, c):
        pair = pl.multiple_of(c & 6, 2)
        return pltpu.make_async_copy(wf.at[c >> 3, :, pl.ds(pair, 2), :], pairs.at[i], sem.at[i])

    def start(t, _):
        tid = template_id(owner, tpb, t)
        for s in range(slots):
            copy(t * slots + s, lists[s, tid]).start()
        return 0

    lax.fori_loop(0, n // slots, start, 0)

    def pick(t, _):
        tid = template_id(owner, tpb, t)
        for g in range(slots // GROUP):
            i = t * slots + g * GROUP
            for k in range(GROUP):
                copy(i + k, 0).wait()
            scr[g, 0 : GROUP * 2 * hb, :] = pairs[pl.ds(i, GROUP), 0:hb].reshape(GROUP * 2 * hb, LANES).astype(f32)
            for k in range(GROUP):
                p = lists[g * GROUP + k, tid] & 1
                hs[pl.ds((i + k) * hb, hb), :] = scr[g, pl.ds(2 * hb * k + p, hb, stride=2), :]
        return 0

    lax.fori_loop(0, n // slots, pick, 0)
    heads[...] = hs[...].astype(bf16)


def energy_kernel(tpb, taps, owner, lists, pairs, halo, rn, a, scr, band):
    slots = lists.shape[0]
    n, blocks = rn.shape[0], rn.shape[1]
    tb = taps // LANES
    half = blocks // 2
    l = lax.broadcasted_iota(i32, (LANES, LANES), 0)
    c = lax.broadcasted_iota(i32, (LANES, LANES), 1)
    before = jnp.where(l < c, 1.0, 0.0).astype(bf16)
    for k, piece in enumerate((jnp.ones_like(before), jnp.ones_like(before), before, before)):
        band[LANES * k : LANES * (k + 1), :] = piece

    def template(t, at):
        tid = template_id(owner, tpb, t)

        def group(g):
            base = t * slots + g * GROUP
            tails = halo[pl.ds(pl.multiple_of(base * tb, GROUP * tb), GROUP * tb), :].astype(f32)
            lhs = []
            for k in range(GROUP):
                i = base + k
                p = lists[g * GROUP + k, tid] & 1
                scr[at * slots + g * GROUP + k, 0 : 2 * blocks, :] = pairs[i].astype(f32)
                scr[at * slots + g * GROUP + k, pl.ds(2 * blocks + p, tb, stride=2), :] = tails[tb * k : tb * (k + 1)]
                q = []
                for v in range(tb + 2):
                    x = scr[at * slots + g * GROUP + k, pl.ds(2 * v + p, half, stride=4), :]
                    a[i, half * v : half * (v + 1), :] = x.astype(bf16)
                    q.append(x * x)
                mid = functools.reduce(jnp.add, q[1:tb])
                for v in range(2):
                    whole, change = mid + q[v * tb], q[v + tb] - q[v]
                    lhs.append(jnp.concatenate(two_parts(whole) + two_parts(change), axis=1))
            e = jnp.dot(jnp.concatenate(lhs, axis=0), band[...], preferred_element_type=f32)
            e = lax.rsqrt(jnp.maximum(e, taps / 4.0))
            for k in range(GROUP):
                rn[base + k] = e[blocks * k : blocks * (k + 1)]

        for g in range(slots // GROUP):
            group(g)

    def step(u, _):
        for at in range(EACH):
            template(u * EACH + at, at)
        return 0

    lax.fori_loop(0, n // slots // EACH, step, 0)


def correlate_kernel(tpb, slots, owner, counts, place, w0, w1, w2, w3, a, rn, *refs):
    outs, (wr, scale, acc) = refs[:-3], refs[-3:]
    w = (w0[...] + w1[...]) + (w2[...] + w3[...])
    n, taps = w.shape
    tb = taps // LANES
    nt = n // slots
    blocks = rn.shape[1]
    half = blocks // 2
    parts = len(outs)
    group = place[0]
    wf = w.astype(f32)
    hi, lo = two_parts(wf * wf)
    ones = jnp.ones((taps, LANES), bf16)
    power = jnp.dot(hi, ones, preferred_element_type=f32) + jnp.dot(lo, ones, preferred_element_type=f32)
    norm = lax.rsqrt(power + FLOOR)
    slot_ids = lax.broadcasted_iota(i32, (slots, LANES), 0) + group * slots
    for t in range(nt):
        count = counts[owner[t // tpb] * tpb + t % tpb]
        scale[t * slots : (t + 1) * slots, :] = jnp.where(slot_ids < count, norm[t * slots : (t + 1) * slots], 0.0)
    row = lax.broadcasted_iota(i32, (LANES, LANES), 0)
    col = lax.broadcasted_iota(i32, (LANES, LANES), 1)
    flip = jnp.where(row + col == LANES - 1, 1.0, 0.0).astype(bf16)
    for j in range(tb):
        wr[j, 0:n, :] = jnp.dot(w[:, LANES * j : LANES * (j + 1)], flip, preferred_element_type=f32)
    own = row >= col
    zero = jnp.zeros((LANES, LANES), bf16)

    def one(i):
        d = [zero]
        for j in range(tb):
            b = jnp.concatenate([wr[j, pl.ds(i, 8, stride=0), :]] * (LANES // 8), axis=0)
            d.append(pltpu.roll(b, 1, axis=1, stride=1, stride_axis=0).astype(bf16))
        d.append(zero)
        band = jnp.concatenate([jnp.where(own, d[j + 1], d[j]) for j in range(tb + 1)], axis=0)
        x = jnp.concatenate([a[i, half * j : half * (j + 2), :] for j in range(tb + 1)], axis=1)
        out = jnp.dot(x, band, preferred_element_type=f32)
        s = scale[pl.ds(i, 8, stride=0), :]
        return out * rn[i] * jnp.concatenate([s] * (blocks // 8), axis=0)

    def template(t, _):
        r = lax.fori_loop(
            0, slots, lambda k, total: total + one(t * slots + k), jnp.zeros((blocks, LANES), f32), unroll=UNROLL
        )
        for v in range(2):
            acc[pl.ds(v * nt + t, half, stride=2 * nt), :] = r[half * v : half * (v + 1)]
        return 0

    lax.fori_loop(0, nt, template, 0)
    per = blocks // parts
    for k, o in enumerate(outs):
        to = (group + k) % parts
        for b in range(per):
            o[:, LANES * b : LANES * (b + 1)] = acc[pl.ds(pl.multiple_of((to * per + b) * nt, 8), nt), :]


def gather(owner, lists, wf4, tpb, tb):
    slots = lists.shape[0]
    n = owner.shape[0] * tpb * slots
    blocks = wf4.shape[1]
    return pl.pallas_call(
        functools.partial(gather_kernel, tpb),
        out_shape=(pltpu.VMEM((n, blocks, 2, LANES), bf16), jax.ShapeDtypeStruct((n * tb, LANES), bf16)),
        grid_spec=pltpu.PrefetchScalarGridSpec(
            num_scalar_prefetch=2,
            in_specs=[pl.BlockSpec(memory_space=pltpu.HBM)],
            out_specs=(vmem_spec(), vmem_spec()),
            scratch_shapes=[
                pltpu.VMEM((slots // GROUP, GROUP * 2 * tb + 8, LANES), f32),
                pltpu.VMEM((n * tb, LANES), f32),
                pltpu.SemaphoreType.DMA((n,)),
            ],
        ),
        compiler_params=pltpu.CompilerParams(vmem_limit_bytes=VMEM_LIMIT),
        name="gather_rows",
    )(in_hbm(owner), in_hbm(lists), in_hbm(wf4))


def energy(owner, lists, pairs, halo, tpb, taps):
    n, blocks = pairs.shape[0], pairs.shape[1] // 2
    tb = taps // LANES
    return pl.pallas_call(
        functools.partial(energy_kernel, tpb, taps),
        out_shape=(pltpu.VMEM((n, blocks, LANES), f32), pltpu.VMEM((n, blocks // 2 * (tb + 2), LANES), bf16)),
        grid_spec=pltpu.PrefetchScalarGridSpec(
            num_scalar_prefetch=2,
            in_specs=[vmem_spec(), vmem_spec()],
            out_specs=(vmem_spec(), vmem_spec()),
            scratch_shapes=[
                pltpu.VMEM((EACH * lists.shape[0], 2 * (blocks + tb) + 8, LANES), f32),
                pltpu.VMEM((4 * LANES, LANES), bf16),
            ],
        ),
        compiler_params=pltpu.CompilerParams(vmem_limit_bytes=VMEM_LIMIT),
        name="window_energy",
    )(in_hbm(owner), in_hbm(lists), pairs, halo)


def correlate(owner, counts, place, ws, a, rn, tpb, slots, parts):
    n, taps = ws[0].shape
    nt = n // slots
    blocks = rn.shape[1]
    return pl.pallas_call(
        functools.partial(correlate_kernel, tpb, slots),
        out_shape=tuple(jax.ShapeDtypeStruct((nt, blocks // parts * LANES), f32) for _ in range(parts)),
        grid_spec=pltpu.PrefetchScalarGridSpec(
            num_scalar_prefetch=3,
            in_specs=[vmem_spec()] * (len(ws) + 2),
            out_specs=tuple(vmem_spec() for _ in range(parts)),
            scratch_shapes=[
                pltpu.VMEM((taps // LANES, n + 8, LANES), f32),
                pltpu.VMEM((n + 8, LANES), f32),
                pltpu.VMEM(((blocks + 2) * nt, LANES), f32),
            ],
        ),
        compiler_params=pltpu.CompilerParams(vmem_limit_bytes=VMEM_LIMIT),
        name="correlate",
    )(in_hbm(owner), in_hbm(counts), place, *ws, a, rn)


def turned(i, dy, dz):
    return ((i // 8 + dy) % 4) * 8 + ((i // 2 + dz) % 4) * 2 + i % 2


def sent(x, to):
    return lax.ppermute(x, "tm", [(i, to(i)) for i in range(32)])


def round_the_ring(x, first):
    turn = lambda k: lambda i: turned(i, 0, k) if (i % 2 == 0) == first else turned(i, k, 0)
    all_four = [x]
    for k in (1, 3, 2):
        all_four.append(sent(x, turn(k)))
    return all_four


def shards(waveforms, templates, channel_lists, channel_counts, owner_rounds):
    c, shard_len = waveforms.shape
    tpb, slots, taps = templates.shape
    rounds = owner_rounds.shape[0]
    n = rounds * tpb * slots
    me = lax.axis_index("tm")
    group = lax.axis_index("tmpl")
    groups = lax.axis_size("tmpl")
    wf4 = waveforms.reshape(c // 8, 8, shard_len // LANES, LANES).transpose(0, 2, 1, 3)
    other = sent(templates, lambda i: i ^ 1)
    owned = (owner_rounds == me)[:, None, None, None]
    paired = (owner_rounds == (me ^ 1))[:, None, None, None]
    nil = jnp.zeros((), templates.dtype)
    waves = jnp.where(owned, templates[None], jnp.where(paired, other[None], nil)).reshape(n, taps)
    waves = functools.reduce(jnp.add, round_the_ring(waves, True))
    lists = channel_lists.T
    pairs, heads = gather(owner_rounds, lists, wf4, tpb, taps // LANES)
    pairs = pairs.reshape(n, -1, LANES)
    halo = lax.ppermute(heads, "tm", [(i, i - 1) for i in range(1, 32)])
    waves = round_the_ring(waves, False)
    rn, a = energy(owner_rounds, lists, pairs, halo, tpb, taps)
    pieces = list(
        correlate(owner_rounds, channel_counts, group.reshape(1), waves, a, rn, tpb, slots, groups)
    )
    for k in range(1, groups):
        pieces[k] = lax.ppermute(pieces[k], "tmpl", [(i, (i + k) % groups) for i in range(groups)])
    return (pieces[0] + pieces[1]) + (pieces[2] + pieces[3])


def solution(mesh):
    in_specs = (P(None, "tm"), P("tm", "tmpl", None), P(None, "tmpl"), P(), P())
    return jax.shard_map(shards, mesh=mesh, in_specs=in_specs, out_specs=P(None, ("tm", "tmpl")), check_vma=False)
```
